128 devices in a mesh: req: 4 (over z), exp: 32 (over y, x, core).
Axes of the slice: x: 4, y: 4, z: 4, core: 2. Of those that a mesh axis runs over, the one named last changes fastest.
Arguments:
- hidden_in: bfloat16 [32, 512, 2048], P('exp'), may hold values from -6 to 6
- cache_keys: bfloat16 [32, 4096, 512], P('exp', None, 'req'), may hold values from -96 to 96
- cache_values: bfloat16 [32, 4096, 512], P('exp', None, 'req'), may hold values from -6 to 6
- cache_len: int32 [32], P('exp'), may hold values from 512 to 4096, as said below
- attn_gain: float32 [2048], replicated, may hold values from 0.25 to 1.75
- w_query: bfloat16 [2048, 4096], P('exp', 'req'), may hold values from -0.125 to 0.125
- w_key: bfloat16 [2048, 512], P('exp', 'req'), may hold values from -0.125 to 0.125
- w_value: bfloat16 [2048, 512], P('exp', 'req'), may hold values from -0.125 to 0.125
- q_gain: float32 [128], replicated, may hold values from 0.5 to 3
- k_gain: float32 [128], replicated, may hold values from 0.25 to 1.75
- w_out: bfloat16 [4096, 2048], P(('req', 'exp')), may hold values from -0.09375 to 0.09375
- moe_gain: float32 [2048], replicated, may hold values from 0.25 to 1.75
- expert_ids: int32 [32, 512, 8], P('exp', 'req'), may hold values from 0 to 127, all different within a row; in each aligned block of 128 rows (0 to 127, 128 to 255, ..., all dimensions but the last counted through in order) at most 12 rows name the same one
- expert_gates: float32 [32, 512, 8], P('exp', 'req'), may hold values from 0.05 to 0.5
- w_gate: bfloat16 [128, 2048, 768], P(('req', 'exp')), may hold values from -0.125 to 0.125
- w_up: bfloat16 [128, 2048, 768], P(('req', 'exp')), may hold values from -0.125 to 0.125
- w_down: bfloat16 [128, 768, 2048], P(('req', 'exp')), may hold values from -0.21875 to 0.21875
Outputs:
- hidden_out: bfloat16 [32, 512, 2048], P('exp', 'req')
- keys_out: bfloat16 [32, 4608, 512], P('exp', None, 'req')
- values_out: bfloat16 [32, 4608, 512], P('exp', None, 'req')
The draws below stay inside these ranges and needn't reach their ends.
Inputs may be any that keep to these rules, and one draw needn't show every extreme that they name: `cache_len`: some request has exactly 4096 cached entries. `expert_ids`: each token names 8 different experts. In each aligned block of 128 tokens no expert is named more than 12 times, a bound that some block reaches.
All inputs are finite; a program needn't handle non-finite values.
Results may differ from the reference program's by a relative error of at most 0.014.
Values may be sent and summed in bfloat16 or wider, within the bound.
A program may use at most 128 MiB of HBM per device.

```python
import math
import jax
import jax.numpy as jnp
import numpy as np
from jax import lax

D = 2048
HEADS = 32
KVH = 4
HD = 128
FF = 768
TOP = 8
CTX = 4096
STRETCH = 512
EXPERTS = 128
REQS = 32
ROWS = 128
CAP = 12


def draw_cache_len(key, part):
    lengths = jax.random.randint(key, (REQS,), CTX // 8, CTX + 1)
    full_index = jax.random.randint(jax.random.fold_in(key, 7), (), 0, REQS)
    return jnp.where(jnp.arange(REQS) == full_index, CTX, lengths).astype(jnp.int32)


def draw_cache_keys(key, part):
    base_draw = jnp.clip(jax.random.normal(key, (REQS, CTX, KVH * HD), jnp.float32), -6.0, 6.0)
    return base_draw.astype(jnp.bfloat16)


def draw_q_gain(key, part):
    gain_vec = jnp.exp(jax.random.uniform(key, (HD,), jnp.float32, jnp.log(0.5), jnp.log(2.0)))
    return gain_vec.astype(jnp.float32)


def block_scale(stream_key, shape, cuts, smallest, top_value):
    def one(position, parts):
        heights = jax.random.uniform(jax.random.fold_in(jax.random.fold_in(stream_key, 6), position), (parts,), jnp.float32, smallest / len(cuts), top_value / len(cuts))
        return jnp.repeat(jnp.exp(heights), shape[position] // parts).reshape((-1,) + (1,) * (len(shape) - position - 1))

    level = one(*cuts[0])
    for cut in cuts[1:]:
        level = level * one(*cut)
    return level


def routed_block(own_key, own, number, rows, number_of, top, reach, slope):
    order = jax.random.permutation(own_key, number_of)
    packed, common = load_shares(number_of, rows * top, reach, slope, True), load_shares(number_of, rows * top, reach, slope, False)
    places = jnp.arange(number_of)

    def named(sizes, rotation):
        used = int((sizes > 0).sum())
        fixed = max(1, used // 4)
        moved = fixed + (places - fixed + rotation * (used - fixed)) % max(1, number_of - fixed)
        return jnp.zeros((number_of,), jnp.int32).at[order[jnp.where(places < fixed, places, moved)]].set(jnp.asarray(sizes, jnp.int32))

    sizes = jnp.where(number % 4 == 0, named(packed, number // 4), named(common, number - number // 4 - 1))
    mixed = jax.random.permutation(jax.random.fold_in(own, 3), number_of)
    giver, sink = mixed[0:number_of // 2 * 2:2], mixed[1:number_of // 2 * 2:2]
    slack = jnp.minimum(sizes[giver] - 1, reach - sizes[sink]) // 2
    slack = jnp.where((giver == order[0]) | (sink == order[0]) | (sizes[sink] == 0), 0, jnp.maximum(slack, 0))
    moved = jax.random.randint(jax.random.fold_in(own, 4), (number_of // 2,), 0, 1 << 20) % (slack + 1)
    sizes = sizes.at[giver].add(-moved).at[sink].add(moved)
    labels = jnp.searchsorted(jnp.cumsum(sizes), jnp.arange(rows * top), side="right").astype(jnp.int32)
    table = labels.reshape(top, rows).T
    table = table[jax.random.permutation(jax.random.fold_in(own, 1), rows)]
    rotation = jax.random.randint(jax.random.fold_in(own, 2), (rows, 1), 0, top)
    return jnp.take_along_axis(table, (jnp.arange(top)[None, :] + rotation) % top, axis=1)


def load_shares(number_of, total, reach, skew, full):
    loads = [(1 << 20) // math.isqrt(grade ** skew) + 1 for grade in range(1, number_of + 1)]
    largest = reach if full else min(reach, max(-(-total // number_of), total * loads[0] // sum(loads)))
    least = 1 if total - largest >= number_of - 1 else 0
    given, rest = [largest] + [least] * (number_of - 1), total - largest - least * (number_of - 1)
    while rest > 0:
        candidates = [i for i in range(1, number_of) if given[i] < largest] or [i for i in range(1, number_of) if given[i] < reach]
        whole, budget = sum([loads[i] for i in candidates]), rest
        for i in candidates:
            addition = min(reach - given[i], max(1, budget * loads[i] // whole), rest)
            given[i] = given[i] + addition
            rest = rest - addition
    return np.array(given)


def normal_values(stream_key, dims, width, limit, shards=(), held_as=jnp.bfloat16):
    factor_of = block_scale(stream_key, dims, shards, -0.22, 0.18) if shards else 1.0
    drawn = jax.random.normal(stream_key, dims, jnp.float32) * width * factor_of
    return jnp.minimum(jnp.maximum(drawn, -limit), limit).astype(held_as)


def setup_inputs(seed: int = 0) -> dict:
    seeds = jax.random.split(jax.random.key(seed), 18)
    hidden_in = normal_values(seeds[0], (REQS, STRETCH, D), 1.0, 6.0, ((0, 32),))
    cache_keys = draw_cache_keys(jax.random.fold_in(seeds[17], 71), 0)
    cache_values = normal_values(seeds[2], (REQS, CTX, KVH * HD), 1.0, 6.0, ((0, 32), (2, 4)))
    cache_len = draw_cache_len(jax.random.fold_in(seeds[17], 71), 0)
    attn_gain = jnp.clip(1.0 + 0.15 * jax.random.normal(seeds[4], (D,), jnp.float32), 0.25, 1.75)
    w_query = normal_values(seeds[5], (D, HEADS * HD), D ** -0.5, 0.125, ((0, 32), (1, 4)))
    w_key = normal_values(seeds[6], (D, KVH * HD), D ** -0.5, 0.125, ((0, 32), (1, 4)))
    w_value = normal_values(seeds[7], (D, KVH * HD), D ** -0.5, 0.125, ((0, 32), (1, 4)))
    q_gain = draw_q_gain(jax.random.fold_in(seeds[17], 71), 0)
    k_gain = jnp.clip(1.0 + 0.15 * jax.random.normal(seeds[9], (HD,), jnp.float32), 0.25, 1.75)
    w_out = normal_values(seeds[10], (HEADS * HD, D), (HEADS * HD) ** -0.5, 0.09375, ((0, 128),))
    moe_gain = jnp.clip(1.0 + 0.15 * jax.random.normal(seeds[11], (D,), jnp.float32), 0.25, 1.75)
    expert_ids_keys = jax.random.split(jax.random.fold_in(seeds[12], 1), REQS * STRETCH // ROWS)
    expert_ids_turns = jax.random.permutation(jax.random.fold_in(seeds[12], 3), REQS * STRETCH // ROWS)
    expert_ids = jax.vmap(lambda own, number: routed_block(jax.random.fold_in(seeds[12], 2), own, number, ROWS, EXPERTS, TOP, CAP, 2))(expert_ids_keys, expert_ids_turns).reshape((REQS, STRETCH, TOP))
    expert_gates = jnp.clip(jnp.exp(math.log(0.5) - 2.3025851 * jax.random.uniform(seeds[13], (REQS, STRETCH, TOP), jnp.float32) ** block_scale(seeds[13], (REQS, STRETCH, TOP), ((0, 32), (1, 4)), -0.2, 0.2)), 0.05, 0.5)
    w_gate = normal_values(seeds[14], (EXPERTS, D, FF), D ** -0.5, 0.125, ((0, 128),))
    w_up = normal_values(seeds[15], (EXPERTS, D, FF), D ** -0.5, 0.125, ((0, 128),))
    w_down = normal_values(seeds[16], (EXPERTS, FF, D), FF ** -0.5, 0.21875, ((0, 128),))
    return {"hidden_in": hidden_in, "cache_keys": cache_keys, "cache_values": cache_values, "cache_len": cache_len, "attn_gain": attn_gain, "w_query": w_query, "w_key": w_key, "w_value": w_value, "q_gain": q_gain, "k_gain": k_gain, "w_out": w_out, "moe_gain": moe_gain, "expert_ids": expert_ids, "expert_gates": expert_gates, "w_gate": w_gate, "w_up": w_up, "w_down": w_down}


EPS = 1e-06
THETA = 1000000.0

def rms_norm(values, gain_vec):
    values = values.astype(jnp.float32)
    factor = lax.rsqrt(lax.optimization_barrier(jnp.mean(values * values, axis=-1, keepdims=True)) + EPS)
    return values * factor * gain_vec.astype(jnp.float32)

def rotate(values, positions):
    half_dim = values.shape[-1] // 2
    frequency = THETA ** (-jnp.arange(half_dim, dtype=jnp.float32) * 2.0 / values.shape[-1])
    angles = positions.astype(jnp.float32)[:, None] * frequency[None, :]
    cosine = jnp.cos(angles)[:, None, :]
    sine_part = jnp.sin(angles)[:, None, :]
    lower_half = values[..., :half_dim]
    upper_half = values[..., half_dim:]
    return jnp.concatenate([lower_half * cosine - upper_half * sine_part, upper_half * cosine + lower_half * sine_part], axis=-1)

def finish(query_proj, key_proj, value_proj, q_gain, k_gain, positions):
    stretch_len = query_proj.shape[0]
    head_dim = q_gain.shape[0]
    queries = rotate(rms_norm(query_proj.reshape(stretch_len, -1, head_dim), q_gain), positions).astype(jnp.bfloat16)
    fresh_keys = rotate(rms_norm(key_proj.reshape(stretch_len, -1, head_dim), k_gain), positions).astype(jnp.bfloat16)
    return (queries.transpose(1, 0, 2), fresh_keys.reshape(stretch_len, -1), value_proj.astype(jnp.bfloat16))

def context(cache, fresh, head_dim):
    joined = jnp.concatenate([cache, fresh], axis=0)
    return joined.reshape(joined.shape[0], -1, head_dim).transpose(1, 0, 2)

def visible(length, context_len, stretch_len):
    key_pos = jnp.arange(context_len + stretch_len, dtype=jnp.int32)[None, :]
    query_pos = jnp.arange(stretch_len, dtype=jnp.int32)[:, None]
    return (key_pos < length) | (key_pos >= context_len) & (key_pos - context_len <= query_pos)

def attend(queries, keys, values, visible_mask):
    group_size = queries.shape[0] // keys.shape[0]
    score_scale = queries.shape[2] ** (-0.5)

    def one_head(operands):
        query_head, head_index = operands
        key_block = keys[head_index // group_size]
        value_block = values[head_index // group_size]
        scores = jnp.dot(query_head, key_block.T, preferred_element_type=jnp.float32) * score_scale
        scores = jnp.where(visible_mask, scores, -1e+30)
        row_peak = lax.optimization_barrier(jnp.max(scores, axis=1, keepdims=True))
        weights = jnp.where(visible_mask, jnp.exp(scores - row_peak), 0.0)
        running = lax.optimization_barrier(jnp.sum(weights, axis=1, keepdims=True))
        mixed = jnp.dot(weights.astype(jnp.bfloat16), value_block, preferred_element_type=jnp.float32)
        return (mixed / running).astype(jnp.bfloat16)
    return lax.map(one_head, (queries, jnp.arange(queries.shape[0], dtype=jnp.int32)))

def append(cache, fresh, length):
    span = cache.shape[0] + fresh.shape[0]
    padded = jnp.concatenate([cache, jnp.zeros_like(fresh)], axis=0)
    kept_rows = jnp.where((jnp.arange(span, dtype=jnp.int32) < length)[:, None], padded, jnp.zeros_like(padded))
    return lax.dynamic_update_slice(kept_rows, fresh, (length.astype(jnp.int32), jnp.zeros((), jnp.int32)))

def reference(hidden_in, cache_keys, cache_values, cache_len, attn_gain, w_query, w_key, w_value, q_gain, k_gain, w_out, moe_gain, expert_ids, expert_gates, w_gate, w_up, w_down):

    def per_request(operands):
        tokens, cache_k, cache_v, length = operands
        normed = rms_norm(tokens, attn_gain).astype(jnp.bfloat16)
        positions = length + jnp.arange(STRETCH, dtype=jnp.int32)
        queries, fresh_keys, fresh_values = finish(jnp.dot(normed, w_query, preferred_element_type=jnp.float32), jnp.dot(normed, w_key, preferred_element_type=jnp.float32), jnp.dot(normed, w_value, preferred_element_type=jnp.float32), q_gain, k_gain, positions)
        visible_mask = visible(length, CTX, STRETCH)
        attended = attend(queries, context(cache_k, fresh_keys, HD), context(cache_v, fresh_values, HD), visible_mask)
        attended = attended.transpose(1, 0, 2).reshape(STRETCH, HEADS * HD)
        mixed = jnp.dot(attended, w_out, preferred_element_type=jnp.float32)
        after_attn = (tokens.astype(jnp.float32) + mixed).astype(jnp.bfloat16)
        return (after_attn, append(cache_k, fresh_keys, length), append(cache_v, fresh_values, length))
    after_attn, keys_out, values_out = lax.map(per_request, (hidden_in, cache_keys, cache_values, cache_len))
    tokens_all = after_attn.reshape(-1, D)
    moe_in = rms_norm(tokens_all, moe_gain).astype(jnp.bfloat16)
    flat_ids = expert_ids.reshape(-1).astype(jnp.int32)
    flat_gates = expert_gates.reshape(-1).astype(jnp.float32)
    pair_order = jnp.argsort(flat_ids, stable=True).astype(jnp.int32)
    counts = jax.ops.segment_sum(jnp.ones_like(flat_ids), flat_ids, num_segments=EXPERTS).astype(jnp.int32)
    starts = (jnp.cumsum(counts) - counts).astype(jnp.int32)
    slot_count = EXPERTS * CAP
    pair_order = jnp.concatenate([pair_order, jnp.zeros((slot_count,), jnp.int32)])

    def serve_rows(accumulated, expert):
        picked = lax.dynamic_slice(pair_order, (starts[expert],), (slot_count,))
        live_slot = jnp.arange(slot_count, dtype=jnp.int32) < counts[expert]
        token_rows = picked // TOP
        block_in = moe_in[token_rows]
        gate_proj = jnp.dot(block_in, w_gate[expert], preferred_element_type=jnp.float32)
        up_proj = jnp.dot(block_in, w_up[expert], preferred_element_type=jnp.float32)
        activated = (jax.nn.silu(gate_proj) * up_proj).astype(jnp.bfloat16)
        produced = jnp.dot(activated, w_down[expert], preferred_element_type=jnp.float32).astype(jnp.bfloat16)
        weight = jnp.where(live_slot, flat_gates[picked], 0.0)
        return (accumulated.at[token_rows].add(produced.astype(jnp.float32) * weight[:, None]), None)
    accumulated, _ = lax.scan(serve_rows, jnp.zeros(tokens_all.shape, jnp.float32), jnp.arange(EXPERTS, dtype=jnp.int32))
    hidden_out = (tokens_all.astype(jnp.float32) + accumulated).astype(jnp.bfloat16).reshape(REQS, STRETCH, D)
    return (hidden_out, keys_out, values_out)
```

```python
import functools
import math

import jax
import jax.numpy as jnp
from jax import lax
from jax.experimental import pallas as pl
from jax.experimental.pallas import tpu as pltpu
from jax.sharding import PartitionSpec as P

EPS = 1e-06
THETA = 1000000.0


def rms_norm(values, gain_vec):
    values = values.astype(jnp.float32)
    factor = lax.rsqrt(jnp.mean(values * values, axis=-1, keepdims=True) + EPS)
    return values * factor * gain_vec


def rotate(values, positions):
    half_dim = values.shape[-1] // 2
    frequency = THETA ** (-jnp.arange(half_dim, dtype=jnp.float32) * 2.0 / values.shape[-1])
    angles = positions.astype(jnp.float32)[:, None] * frequency[None, :]
    cosine = jnp.cos(angles)[:, None, :]
    sine_part = jnp.sin(angles)[:, None, :]
    lower_half = values[..., :half_dim]
    upper_half = values[..., half_dim:]
    return jnp.concatenate(
        [
            lower_half * cosine - upper_half * sine_part,
            upper_half * cosine + lower_half * sine_part,
        ],
        axis=-1,
    )


def finish(query_proj, key_proj, value_proj, q_gain, k_gain, positions):
    stretch_len = query_proj.shape[0]
    head_dim = q_gain.shape[0]
    queries = rotate(
        rms_norm(query_proj.reshape(stretch_len, -1, head_dim), q_gain), positions
    ).astype(jnp.bfloat16)
    fresh_keys = rotate(
        rms_norm(key_proj.reshape(stretch_len, -1, head_dim), k_gain), positions
    ).astype(jnp.bfloat16)
    return (
        queries.transpose(1, 0, 2),
        fresh_keys.reshape(stretch_len, -1),
        value_proj.astype(jnp.bfloat16),
    )


def attention_body(exp_scale, len_ref, q_ref, k_ref, v_ref, fk_ref, fv_ref, o_ref, kaug, vaug):
    block = pl.program_id(0)
    length = len_ref[0]
    heads, tokens, width = q_ref.shape
    cached = k_ref.shape[0]
    fresh = fk_ref.shape[0]

    @pl.when(block == 0)
    def _():
        kaug[0:cached, 0:width] = k_ref[...]
        kaug[cached:, 0:width] = fk_ref[...]
        row = lax.broadcasted_iota(jnp.int32, (cached + fresh, width), 0)
        lane = lax.broadcasted_iota(jnp.int32, (cached + fresh, width), 1)
        hidden = (lane == 0) & (row >= length) & (row < cached)
        kaug[:, width:] = jnp.where(hidden, -1e30, 0.0).astype(jnp.bfloat16)
        vaug[0:cached, 0:width] = v_ref[...]
        vaug[cached:, 0:width] = fv_ref[...]
        vaug[:, width:] = jnp.ones((cached + fresh, width), jnp.bfloat16)

    rows = heads * tokens
    queries = q_ref[...].reshape(rows, width)
    widened = jnp.concatenate([queries, jnp.ones((rows, width), jnp.bfloat16)], axis=1)
    dims = (((1,), (1,)), ((), ()))
    old = lax.dot_general(widened, kaug[0:cached, :], dims, preferred_element_type=jnp.float32)
    new = lax.dot_general(
        queries, kaug[cached:, 0:width], dims, preferred_element_type=jnp.float32
    )
    token = lax.broadcasted_iota(jnp.int32, (rows, fresh), 0) % tokens + block * tokens
    new = jnp.where(lax.broadcasted_iota(jnp.int32, (rows, fresh), 1) <= token, new, -1e30)
    peak = jnp.maximum(
        jnp.max(old, axis=1, keepdims=True), jnp.max(new, axis=1, keepdims=True)
    )
    old = jnp.exp2((old - peak) * exp_scale).astype(jnp.bfloat16)
    new = jnp.exp2((new - peak) * exp_scale).astype(jnp.bfloat16)
    mixed = jnp.dot(old, vaug[0:cached, :], preferred_element_type=jnp.float32) + jnp.dot(
        new, vaug[cached:, :], preferred_element_type=jnp.float32
    )
    mixed = (mixed[:, :width] / mixed[:, width:]).astype(jnp.bfloat16)
    for head in range(heads):
        o_ref[:, head * width : (head + 1) * width] = mixed[head * tokens : (head + 1) * tokens]


def attend(queries, cache_k, cache_v, fresh_k, fresh_v, length, tokens=128):
    heads, stretch_len, width = queries.shape
    span = cache_k.shape[0] + fresh_k.shape[0]
    whole = lambda arr: pl.BlockSpec(arr.shape, lambda i, n: (0, 0))
    return pl.pallas_call(
        functools.partial(attention_body, width ** -0.5 * math.log2(math.e)),
        out_shape=jax.ShapeDtypeStruct((stretch_len, heads * width), jnp.bfloat16),
        grid_spec=pltpu.PrefetchScalarGridSpec(
            num_scalar_prefetch=1,
            grid=(stretch_len // tokens,),
            in_specs=[
                pl.BlockSpec((heads, tokens, width), lambda i, n: (0, i, 0)),
                whole(cache_k),
                whole(cache_v),
                whole(fresh_k),
                whole(fresh_v),
            ],
            out_specs=pl.BlockSpec((tokens, heads * width), lambda i, n: (i, 0)),
            scratch_shapes=[
                pltpu.VMEM((span, 2 * width), jnp.bfloat16),
                pltpu.VMEM((span, 2 * width), jnp.bfloat16),
            ],
        ),
        compiler_params=pltpu.CompilerParams(vmem_limit_bytes=58 << 20),
        name="attend",
    )(length, queries, cache_k, cache_v, fresh_k, fresh_v)


def append(cache, fresh, length):
    span = cache.shape[0] + fresh.shape[0]
    padded = jnp.concatenate([cache, jnp.zeros_like(fresh)], axis=0)
    kept_rows = jnp.where(
        (jnp.arange(span, dtype=jnp.int32) < length)[:, None], padded, jnp.zeros_like(padded)
    )
    return lax.dynamic_update_slice(kept_rows, fresh, (length, jnp.zeros((), jnp.int32)))


def body(
    hidden_in,
    cache_keys,
    cache_values,
    cache_len,
    attn_gain,
    w_query,
    w_key,
    w_value,
    q_gain,
    k_gain,
    w_out,
    moe_gain,
    expert_ids,
    expert_gates,
    w_gate,
    w_up,
    w_down,
):
    tokens = hidden_in[0]
    stretch_len = tokens.shape[0]
    model_width = tokens.shape[1]
    length = cache_len[0]
    head_dim = q_gain.shape[0]
    normed = rms_norm(tokens, attn_gain).astype(jnp.bfloat16)
    widths = (w_query.shape[1], w_key.shape[1], w_value.shape[1])
    w_all = lax.all_gather(
        jnp.concatenate([w_query, w_key, w_value], axis=1), "exp", axis=0, tiled=True
    )
    proj = jnp.dot(normed, w_all, preferred_element_type=jnp.float32)
    query_proj = proj[:, : widths[0]]
    key_proj = proj[:, widths[0] : widths[0] + widths[1]]
    value_proj = proj[:, widths[0] + widths[1] :]
    positions = length + jnp.arange(stretch_len, dtype=jnp.int32)
    queries, fresh_keys, fresh_values = finish(
        query_proj, key_proj, value_proj, q_gain, k_gain, positions
    )
    attended = attend(queries, cache_keys[0], cache_values[0], fresh_keys, fresh_values, cache_len)
    groups = lax.axis_size("req")
    row_count = stretch_len // groups
    offset = lax.axis_index("req") * row_count
    block_in = attended
    partial_out = jnp.dot(
        block_in,
        lax.all_gather(w_out, "exp", axis=0, tiled=True),
        preferred_element_type=jnp.float32,
    )
    mixed = lax.psum_scatter(
        partial_out.astype(jnp.bfloat16), "req", scatter_dimension=0, tiled=True
    ).astype(jnp.float32)
    resident = lax.dynamic_slice_in_dim(tokens, offset, row_count, 0)
    after_attn = (resident.astype(jnp.float32) + mixed).astype(jnp.bfloat16)
    moe_in = rms_norm(after_attn, moe_gain).astype(jnp.bfloat16)
    routes = expert_ids[0]
    top_k = routes.shape[1]
    experts = groups * lax.axis_size("exp")
    capacity = 3 * top_k * row_count // (2 * experts)
    flat_ids = routes.reshape(-1)
    onehot = (flat_ids[:, None] == jnp.arange(experts, dtype=jnp.int32)[None, :]).astype(jnp.int32)
    slots = jnp.sum((jnp.cumsum(onehot, axis=0) - 1) * onehot, axis=1)
    target = flat_ids * capacity + slots
    sources = jnp.arange(row_count * top_k, dtype=jnp.int32) // top_k
    outgoing = (
        jnp.zeros((experts * capacity, model_width), jnp.bfloat16).at[target].set(moe_in[sources])
    )
    outgoing = outgoing.reshape(experts, capacity, model_width)
    block_in = lax.all_to_all(outgoing, ("req", "exp"), split_axis=0, concat_axis=0, tiled=True)
    flat_rows = block_in.reshape(-1, model_width)
    gate_proj = jnp.dot(flat_rows, w_gate[0], preferred_element_type=jnp.float32)
    up_proj = jnp.dot(flat_rows, w_up[0], preferred_element_type=jnp.float32)
    activated = (jax.nn.silu(gate_proj) * up_proj).astype(jnp.bfloat16)
    produced = jnp.dot(activated, w_down[0], preferred_element_type=jnp.float32).astype(
        jnp.bfloat16
    )
    returned = lax.all_to_all(
        produced.reshape(block_in.shape), ("req", "exp"), split_axis=0, concat_axis=0, tiled=True
    )
    picked = returned.reshape(experts * capacity, model_width)[target].reshape(
        row_count, top_k, model_width
    )
    combined = jnp.sum(picked.astype(jnp.float32) * expert_gates[0][:, :, None], axis=1)
    result_rows = (after_attn.astype(jnp.float32) + combined).astype(jnp.bfloat16)
    keys_out = append(cache_keys[0], fresh_keys, length)
    values_out = append(cache_values[0], fresh_values, length)
    return (result_rows[None], keys_out[None], values_out[None])


def solution(mesh):
    placed = (
        P("exp", None, None),
        P("exp", None, "req"),
        P("exp", None, "req"),
        P("exp"),
        P(),
        P("exp", "req"),
        P("exp", "req"),
        P("exp", "req"),
        P(),
        P(),
        P(("req", "exp"), None),
        P(),
        P("exp", "req", None),
        P("exp", "req", None),
        P(("req", "exp"), None, None),
        P(("req", "exp"), None, None),
        P(("req", "exp"), None, None),
    )
    return jax.shard_map(
        body,
        mesh=mesh,
        in_specs=placed,
        out_specs=(P("exp", "req", None), P("exp", None, "req"), P("exp", None, "req")),
        check_vma=False,
    )
```

```python
import functools
import math

import jax
import jax.numpy as jnp
from jax import lax
from jax.experimental import pallas as pl
from jax.experimental.pallas import tpu as pltpu
from jax.sharding import PartitionSpec as P

EPS = 1e-06
THETA = 1000000.0


def rms_norm(values, gain_vec):
    values = values.astype(jnp.float32)
    factor = lax.rsqrt(jnp.mean(values * values, axis=-1, keepdims=True) + EPS)
    return values * factor * gain_vec


def rotate(values, positions):
    half_dim = values.shape[-1] // 2
    frequency = THETA ** (-jnp.arange(half_dim, dtype=jnp.float32) * 2.0 / values.shape[-1])
    angles = positions.astype(jnp.float32)[:, None] * frequency[None, :]
    cosine = jnp.cos(angles)[:, None, :]
    sine_part = jnp.sin(angles)[:, None, :]
    lower_half = values[..., :half_dim]
    upper_half = values[..., half_dim:]
    return jnp.concatenate(
        [
            lower_half * cosine - upper_half * sine_part,
            upper_half * cosine + lower_half * sine_part,
        ],
        axis=-1,
    )


def finish(query_proj, key_proj, value_proj, q_gain, k_gain, positions):
    stretch_len = query_proj.shape[0]
    head_dim = q_gain.shape[0]
    queries = rotate(
        rms_norm(query_proj.reshape(stretch_len, -1, head_dim), q_gain), positions
    ).astype(jnp.bfloat16)
    fresh_keys = rotate(
        rms_norm(key_proj.reshape(stretch_len, -1, head_dim), k_gain), positions
    ).astype(jnp.bfloat16)
    return (
        queries.transpose(1, 0, 2),
        fresh_keys.reshape(stretch_len, -1),
        value_proj.astype(jnp.bfloat16),
    )


def attention_body(exp_scale, len_ref, q_ref, k_ref, v_ref, fk_ref, fv_ref, o_ref, kaug, vaug):
    block = pl.program_id(0)
    length = len_ref[0]
    heads, tokens, width = q_ref.shape
    cached = k_ref.shape[0]
    fresh = fk_ref.shape[0]

    @pl.when(block == 0)
    def _():
        kaug[0:cached, 0:width] = k_ref[...]
        kaug[cached:, 0:width] = fk_ref[...]
        row = lax.broadcasted_iota(jnp.int32, (cached + fresh, width), 0)
        lane = lax.broadcasted_iota(jnp.int32, (cached + fresh, width), 1)
        hidden = (lane == 0) & (row >= length) & (row < cached)
        kaug[:, width:] = jnp.where(hidden, -1e30, 0.0).astype(jnp.bfloat16)
        vaug[0:cached, 0:width] = v_ref[...]
        vaug[cached:, 0:width] = fv_ref[...]
        vaug[:, width:] = jnp.ones((cached + fresh, width), jnp.bfloat16)

    rows = heads * tokens
    queries = q_ref[...].reshape(rows, width)
    widened = jnp.concatenate([queries, jnp.ones((rows, width), jnp.bfloat16)], axis=1)
    dims = (((1,), (1,)), ((), ()))
    old = lax.dot_general(widened, kaug[0:cached, :], dims, preferred_element_type=jnp.float32)
    new = lax.dot_general(
        queries, kaug[cached:, 0:width], dims, preferred_element_type=jnp.float32
    )
    token = lax.broadcasted_iota(jnp.int32, (rows, fresh), 0) % tokens + block * tokens
    new = jnp.where(lax.broadcasted_iota(jnp.int32, (rows, fresh), 1) <= token, new, -1e30)
    peak = jnp.maximum(
        jnp.max(old, axis=1, keepdims=True), jnp.max(new, axis=1, keepdims=True)
    )
    old = jnp.exp2((old - peak) * exp_scale).astype(jnp.bfloat16)
    new = jnp.exp2((new - peak) * exp_scale).astype(jnp.bfloat16)
    mixed = jnp.dot(old, vaug[0:cached, :], preferred_element_type=jnp.float32) + jnp.dot(
        new, vaug[cached:, :], preferred_element_type=jnp.float32
    )
    mixed = (mixed[:, :width] / mixed[:, width:]).astype(jnp.bfloat16)
    for head in range(heads):
        o_ref[:, head * width : (head + 1) * width] = mixed[head * tokens : (head + 1) * tokens]


def attend(queries, cache_k, cache_v, fresh_k, fresh_v, length, tokens=128):
    heads, stretch_len, width = queries.shape
    span = cache_k.shape[0] + fresh_k.shape[0]
    whole = lambda arr: pl.BlockSpec(arr.shape, lambda i, n: (0, 0))
    return pl.pallas_call(
        functools.partial(attention_body, width ** -0.5 * math.log2(math.e)),
        out_shape=jax.ShapeDtypeStruct((stretch_len, heads * width), jnp.bfloat16),
        grid_spec=pltpu.PrefetchScalarGridSpec(
            num_scalar_prefetch=1,
            grid=(stretch_len // tokens,),
            in_specs=[
                pl.BlockSpec((heads, tokens, width), lambda i, n: (0, i, 0)),
                whole(cache_k),
                whole(cache_v),
                whole(fresh_k),
                whole(fresh_v),
            ],
            out_specs=pl.BlockSpec((tokens, heads * width), lambda i, n: (i, 0)),
            scratch_shapes=[
                pltpu.VMEM((span, 2 * width), jnp.bfloat16),
                pltpu.VMEM((span, 2 * width), jnp.bfloat16),
            ],
        ),
        compiler_params=pltpu.CompilerParams(vmem_limit_bytes=58 << 20),
        name="attend",
    )(length, queries, cache_k, cache_v, fresh_k, fresh_v)


MESH_ID = pl.DeviceIdType.MESH
SPLIT = 4


def place():
    group = lax.axis_index("exp")
    return lax.axis_index("req"), group // 8, (group // 2) % 4, group % 2


def ring_peer(part, step, where):
    plane, row, column, core = where
    if part == 0:
        spot = (row + step) % 4
        return (plane, spot * 8 + column * 2 + core), spot
    spot = (column + step) % 4
    return (plane, row * 8 + spot * 2 + core), spot


def swap_peer(part, step, where):
    plane, row, column, core = where
    side = (core + step) % 2
    if part == 0:
        spot = (column + step // 2) % 4
        return (plane, row * 8 + spot * 2 + side), spot * 2 + side
    spot = (row + step // 2) % 4
    return (plane, spot * 8 + column * 2 + side), spot * 2 + side


def plane_peer(step, where):
    plane, row, column, core = where
    spot = (plane + step) % 4
    return (spot, row * 8 + column * 2 + core), spot


def greet(where):
    barrier = pltpu.get_barrier_semaphore()
    peers = [plane_peer(step, where)[0] for step in (1, 2, 3)]
    peers += [swap_peer(0, step, where)[0] for step in range(1, 8)]
    peers += [swap_peer(1, step, where)[0] for step in range(2, 8)]
    for peer in peers:
        pl.semaphore_signal(barrier, inc=1, device_id=peer, device_id_type=MESH_ID)
    pl.semaphore_wait(barrier, len(peers))


def remote(src, dst, send_sem, recv_sem, peer):
    return pltpu.make_async_remote_copy(
        src_ref=src,
        dst_ref=dst,
        send_sem=send_sem,
        recv_sem=recv_sem,
        device_id=peer,
        device_id_type=MESH_ID,
    )


def serve_body(
    rows_ref, map_ref, gate_ref, up_ref, down_ref, made_ref, weigh_ref,
    tokens, maps, pick, outbox, inbox, w_gate, w_up, w_down, made,
    z_send, z_recv, b_send, b_recv, c_send, c_recv, m_send, m_recv, n_send, n_recv,
    local_sem, w_sem, made_sem, weigh_sem,
):
    where = place()
    plane, row, column, core = where
    at = (row, column)
    chunk = tokens.shape[-1]
    loads = [
        pltpu.make_async_copy(src.at[0], dst, w_sem.at[i])
        for i, (src, dst) in enumerate(((gate_ref, w_gate), (up_ref, w_up), (down_ref, w_down)))
    ]
    for load in loads:
        load.start()
    for part in range(2):
        maps[part, at[part], plane] = map_ref[plane]
    for q in range(SPLIT):
        tokens[q, at[q % 2], plane] = rows_ref[:, q * chunk : (q + 1) * chunk]
    greet(where)
    sent = []

    def send(copy):
        copy.start()
        sent.append(copy)

    for part in range(2):
        for step in (1, 2, 3):
            peer, spot = plane_peer(step, where)
            send(remote(
                map_ref.at[spot], maps.at[part, at[part], plane],
                m_send.at[part, step], m_recv.at[part, plane], peer,
            ))
    for q in range(SPLIT):
        for step in (1, 2, 3):
            peer, spot = plane_peer(step, where)
            send(remote(
                rows_ref.at[:, q * chunk : (q + 1) * chunk], tokens.at[q, at[q % 2], plane],
                z_send.at[q, step], z_recv.at[q, plane], peer,
            ))
    for part in range(2):
        for step in (1, 2, 3):
            peer, spot = plane_peer(step, where)
            slot = maps.at[part, at[part], spot]
            remote(slot, slot, m_send.at[part, step], m_recv.at[part, spot], peer).wait_recv()
        for step in (1, 2, 3):
            peer, spot = ring_peer(part, step, where)
            slot = maps.at[part, at[part]]
            send(remote(slot, slot, n_send.at[part, step], n_recv.at[part, at[part]], peer))
    for q in range(SPLIT):
        part = q % 2
        for step in (1, 2, 3):
            peer, spot = plane_peer(step, where)
            slot = tokens.at[q, at[part], spot]
            remote(slot, slot, z_send.at[q, step], z_recv.at[q, spot], peer).wait_recv()
        for step in (1, 2, 3):
            peer, spot = ring_peer(part, step, where)
            slot = tokens.at[q, at[part]]
            send(remote(slot, slot, b_send.at[q, step], b_recv.at[q, at[part]], peer))

    slots = pick.shape[2] // 32
    group = 4 * slots
    width = pick.shape[3]
    r_id = lax.broadcasted_iota(jnp.int32, (group, width), 0)
    c_id = lax.broadcasted_iota(jnp.int32, (group, width), 1)
    wanted = jnp.where(
        r_id // slots == c_id // (width // 4), (r_id % slots + 1).astype(jnp.float32), -1.0
    )
    for part in range(2):
        for step in (1, 2, 3):
            peer, spot = ring_peer(part, step, where)
            slot = maps.at[part, spot]
            remote(slot, slot, n_send.at[part, step], n_recv.at[part, spot], peer).wait_recv()

        def choose(b, carry, part=part):
            weighed = []
            for i in range(8):
                local = row * 8 + i if part == 0 else (i // 2) * 8 + column * 2 + i % 2
                named = jnp.concatenate(
                    [maps[part, b, z, pl.ds(local, 1), :] for z in range(4)], axis=1
                )
                gates = jnp.concatenate(
                    [maps[part, b, z, pl.ds(32 + local, 1), :] for z in range(4)], axis=1
                )
                hit = wanted == named
                pick[part, b, i * group : (i + 1) * group, :] = jnp.where(hit, 1.0, 0.0).astype(
                    jnp.bfloat16
                )
                weighed.append(jnp.where(hit, gates, 0.0))
            made_of = jnp.concatenate(weighed, axis=0)
            weigh_ref[part, b] = made_of.T.astype(jnp.bfloat16)
            return carry

        lax.fori_loop(0, 4, choose, 0)

    mine = (column * 2 + core, row * 2 + core)
    locals_ = []
    for q in range(SPLIT):
        part = q % 2
        cols = pl.ds(q * chunk, chunk)
        for step in (1, 2, 3):
            peer, spot = ring_peer(part, step, where)
            slot = tokens.at[q, spot]
            remote(slot, slot, b_send.at[q, step], b_recv.at[q, spot], peer).wait_recv()

        def gather(b, carry, q=q, part=part):
            rows = tokens[q, b].reshape(width, chunk)
            chosen = jnp.dot(pick[part, b], rows, preferred_element_type=jnp.float32)
            outbox[q, :, b] = chosen.astype(jnp.bfloat16).reshape(8, group, chunk)
            return carry

        lax.fori_loop(0, 4, gather, 0)

        def target(row_, column_, core_):
            if part == 0:
                return inbox.at[:, column_, core_, :, cols]
            return inbox.at[row_, :, core_, :, cols]

        for step in range(2, 8):
            peer, spot = swap_peer(part, step, where)
            send(remote(
                outbox.at[q, spot], target(row, column, core),
                c_send.at[q, step], c_recv.at[q, mine[part]], peer,
            ))
        peer, spot = swap_peer(part, 1, where)
        send(remote(
            outbox.at[q, spot], target(row, column, core),
            c_send.at[q, 1], c_recv.at[q, mine[part]], peer,
        ))
        own = pltpu.make_async_copy(
            outbox.at[q, mine[part]], target(row, column, core), local_sem.at[q]
        )
        own.start()
        locals_.append(own)
    for own in locals_:
        own.wait()
    for q in range(SPLIT):
        part = q % 2
        cols = pl.ds(q * chunk, chunk)
        for step in range(1, 8):
            peer, spot = swap_peer(part, step, where)
            if part == 0:
                slot = inbox.at[:, spot // 2, spot % 2, :, cols]
            else:
                slot = inbox.at[spot // 2, :, spot % 2, :, cols]
            remote(
                outbox.at[q, spot], slot, c_send.at[q, step], c_recv.at[q, spot], peer
            ).wait_recv()
    for load in loads:
        load.wait()

    def expert(r, carry):
        x = inbox[r].reshape(8 * group, inbox.shape[-1])
        gate = jnp.dot(x, w_gate[...], preferred_element_type=jnp.float32)
        up = jnp.dot(x, w_up[...], preferred_element_type=jnp.float32)
        hidden = (gate / (1.0 + jnp.exp(-gate)) * up).astype(jnp.bfloat16)
        out = jnp.dot(hidden, w_down[...], preferred_element_type=jnp.float32)
        made[r] = out.astype(jnp.bfloat16).reshape(made.shape[1:])
        pltpu.make_async_copy(made.at[r], made_ref.at[r], made_sem.at[r]).start()
        return carry

    lax.fori_loop(0, 4, expert, 0)
    for r in range(4):
        pltpu.make_async_copy(made.at[r], made_ref.at[r], made_sem.at[r]).wait()
    for copy in sent:
        copy.wait_send()


def serve(rows, maps, w_gate, w_up, w_down, capacity):
    tokens, width = rows.shape
    hidden = w_gate.shape[2]
    chunk = width // SPLIT
    group = 4 * capacity
    bf = jnp.bfloat16
    dma = pltpu.SemaphoreType.DMA
    vmem = pl.BlockSpec(memory_space=pltpu.VMEM)
    anywhere = pl.BlockSpec(memory_space=pl.ANY)
    return pl.pallas_call(
        serve_body,
        out_shape=(
            jax.ShapeDtypeStruct((4, 4, 2, group, width), bf),
            jax.ShapeDtypeStruct((2, 4, 4 * tokens, 8 * group), bf),
        ),
        in_specs=[vmem, vmem, anywhere, anywhere, anywhere],
        out_specs=(anywhere, vmem),
        scratch_shapes=[
            pltpu.VMEM((SPLIT, 4, 4, tokens, chunk), bf),
            pltpu.VMEM((2, 4, 4) + maps.shape[1:], jnp.float32),
            pltpu.VMEM((2, 4, 8 * group, 4 * tokens), bf),
            pltpu.VMEM((SPLIT, 8, 4, group, chunk), bf),
            pltpu.VMEM((4, 4, 2, group, width), bf),
            pltpu.VMEM((width, hidden), bf),
            pltpu.VMEM((width, hidden), bf),
            pltpu.VMEM((hidden, width), bf),
            pltpu.VMEM((4, 4, 2, group, width), bf),
            dma((SPLIT, 4)), dma((SPLIT, 4)),
            dma((SPLIT, 4)), dma((SPLIT, 4)),
            dma((SPLIT, 8)), dma((SPLIT, 8)),
            dma((2, 4)), dma((2, 4)), dma((2, 4)), dma((2, 4)),
            dma((SPLIT,)), dma((3,)), dma((4,)), dma((1,)),
        ],
        compiler_params=pltpu.CompilerParams(
            collective_id=0, has_side_effects=True, vmem_limit_bytes=62 << 20
        ),
        name="serve",
    )(rows, maps, w_gate, w_up, w_down)


def combine_body(
    made_ref, weigh_ref, base_ref, out_ref,
    back, share, shares, total, totals,
    c_send, c_recv, b_send, b_recv, z_send, z_recv, local_sem,
):
    where = place()
    plane, row, column, core = where
    at = (row, column)
    mine = (column * 2 + core, row * 2 + core)
    chunk = total.shape[-1]
    tokens = base_ref.shape[0]
    greet(where)
    sent = []

    def send(copy):
        copy.start()
        sent.append(copy)

    for q in range(SPLIT):
        part = q % 2
        cols = pl.ds(q * chunk, chunk)

        def source(spot):
            if part == 0:
                return made_ref.at[:, spot // 2, spot % 2, :, cols]
            return made_ref.at[spot // 2, :, spot % 2, :, cols]

        for step in (2, 3, 4, 5, 6, 7, 1):
            peer, spot = swap_peer(part, step, where)
            send(remote(
                source(spot), back.at[q, :, mine[part]],
                c_send.at[q, step], c_recv.at[q, mine[part]], peer,
            ))
        pltpu.make_async_copy(
            source(mine[part]), back.at[q, :, mine[part]], local_sem.at[q]
        ).start()
    for q in range(SPLIT):
        part = q % 2
        for step in range(1, 8):
            peer, spot = swap_peer(part, step, where)
            slot = back.at[q, :, spot]
            remote(slot, slot, c_send.at[q, step], c_recv.at[q, spot], peer).wait_recv()
        slot = back.at[q, :, mine[part]]
        pltpu.make_async_copy(slot, slot, local_sem.at[q]).wait()

        def weigh(b, carry, q=q, part=part):
            rows = back[q, b].reshape(weigh_ref.shape[-1], chunk)
            share[q, b] = jnp.dot(
                weigh_ref[part, b], rows, preferred_element_type=jnp.float32
            ).astype(jnp.bfloat16)
            return carry

        lax.fori_loop(0, 4, weigh, 0)
        for step in (1, 2, 3):
            peer, spot = ring_peer(part, step, where)
            send(remote(
                share.at[q, spot], shares.at[q, at[part]],
                b_send.at[q, step], b_recv.at[q, at[part]], peer,
            ))
    for q in range(SPLIT):
        part = q % 2
        added = share[q, at[part]].astype(jnp.float32)
        for step in (1, 2, 3):
            peer, spot = ring_peer(part, step, where)
            slot = shares.at[q, spot]
            remote(slot, slot, b_send.at[q, step], b_recv.at[q, spot], peer).wait_recv()
            added = added + shares[q, spot].astype(jnp.float32)
        total[q] = added.astype(jnp.bfloat16).reshape(4, tokens, chunk)
        for step in (1, 2, 3):
            peer, spot = plane_peer(step, where)
            send(remote(
                total.at[q, spot], totals.at[q, plane],
                z_send.at[q, step], z_recv.at[q, plane], peer,
            ))
    for q in range(SPLIT):
        cols = slice(q * chunk, (q + 1) * chunk)
        added = total[q, plane].astype(jnp.float32)
        for step in (1, 2, 3):
            peer, spot = plane_peer(step, where)
            slot = totals.at[q, spot]
            remote(slot, slot, z_send.at[q, step], z_recv.at[q, spot], peer).wait_recv()
            added = added + totals[q, spot].astype(jnp.float32)
        out_ref[:, cols] = (base_ref[:, cols].astype(jnp.float32) + added).astype(jnp.bfloat16)
    for copy in sent:
        copy.wait_send()


def combine(made, weigh, base):
    tokens, width = base.shape
    chunk = width // SPLIT
    group = made.shape[3]
    bf = jnp.bfloat16
    dma = pltpu.SemaphoreType.DMA
    vmem = pl.BlockSpec(memory_space=pltpu.VMEM)
    return pl.pallas_call(
        combine_body,
        out_shape=jax.ShapeDtypeStruct(base.shape, bf),
        in_specs=[pl.BlockSpec(memory_space=pl.ANY), vmem, vmem],
        out_specs=vmem,
        scratch_shapes=[
            pltpu.VMEM((SPLIT, 4, 8, group, chunk), bf),
            pltpu.VMEM((SPLIT, 4, 4 * tokens, chunk), bf),
            pltpu.VMEM((SPLIT, 4, 4 * tokens, chunk), bf),
            pltpu.VMEM((SPLIT, 4, tokens, chunk), bf),
            pltpu.VMEM((SPLIT, 4, tokens, chunk), bf),
            dma((SPLIT, 8)), dma((SPLIT, 8)),
            dma((SPLIT, 4)), dma((SPLIT, 4)),
            dma((SPLIT, 4)), dma((SPLIT, 4)), dma((SPLIT,)),
        ],
        compiler_params=pltpu.CompilerParams(
            collective_id=1, has_side_effects=True, vmem_limit_bytes=62 << 20
        ),
        name="combine",
    )(made, weigh, base)


def routing_maps(routes, gates, experts, planes):
    rows = routes.shape[0]
    ids = routes.T[None, :, :]
    hit = ids == jnp.arange(experts, dtype=jnp.int32)[:, None, None]
    named = jnp.sum(hit.astype(jnp.float32), axis=1)
    weight = jnp.sum(jnp.where(hit, gates.T[None, :, :], 0.0), axis=1)
    upto = (
        jnp.arange(rows, dtype=jnp.int32)[:, None] <= jnp.arange(rows, dtype=jnp.int32)[None, :]
    )
    order = jnp.dot(
        named.astype(jnp.bfloat16), upto.astype(jnp.bfloat16), preferred_element_type=jnp.float32
    )
    slot = order * named
    per_plane = experts // planes
    return jnp.concatenate(
        [slot.reshape(planes, per_plane, rows), weight.reshape(planes, per_plane, rows)], axis=1
    )


def append(cache, fresh, length):
    span = cache.shape[0] + fresh.shape[0]
    padded = jnp.concatenate([cache, jnp.zeros_like(fresh)], axis=0)
    kept_rows = jnp.where(
        (jnp.arange(span, dtype=jnp.int32) < length)[:, None], padded, jnp.zeros_like(padded)
    )
    return lax.dynamic_update_slice(kept_rows, fresh, (length, jnp.zeros((), jnp.int32)))


def body(
    hidden_in,
    cache_keys,
    cache_values,
    cache_len,
    attn_gain,
    w_query,
    w_key,
    w_value,
    q_gain,
    k_gain,
    w_out,
    moe_gain,
    expert_ids,
    expert_gates,
    w_gate,
    w_up,
    w_down,
):
    tokens = hidden_in[0]
    stretch_len = tokens.shape[0]
    model_width = tokens.shape[1]
    length = cache_len[0]
    head_dim = q_gain.shape[0]
    normed = rms_norm(tokens, attn_gain).astype(jnp.bfloat16)
    widths = (w_query.shape[1], w_key.shape[1], w_value.shape[1])
    w_all = lax.all_gather(
        jnp.concatenate([w_query, w_key, w_value], axis=1), "exp", axis=0, tiled=True
    )
    proj = jnp.dot(normed, w_all, preferred_element_type=jnp.float32)
    query_proj = proj[:, : widths[0]]
    key_proj = proj[:, widths[0] : widths[0] + widths[1]]
    value_proj = proj[:, widths[0] + widths[1] :]
    positions = length + jnp.arange(stretch_len, dtype=jnp.int32)
    queries, fresh_keys, fresh_values = finish(
        query_proj, key_proj, value_proj, q_gain, k_gain, positions
    )
    attended = attend(queries, cache_keys[0], cache_values[0], fresh_keys, fresh_values, cache_len)
    groups = lax.axis_size("req")
    row_count = stretch_len // groups
    offset = lax.axis_index("req") * row_count
    block_in = attended
    partial_out = jnp.dot(
        block_in,
        lax.all_gather(w_out, "exp", axis=0, tiled=True),
        preferred_element_type=jnp.float32,
    )
    mixed = lax.psum_scatter(
        partial_out.astype(jnp.bfloat16), "req", scatter_dimension=0, tiled=True
    ).astype(jnp.float32)
    resident = lax.dynamic_slice_in_dim(tokens, offset, row_count, 0)
    after_attn = (resident.astype(jnp.float32) + mixed).astype(jnp.bfloat16)
    moe_in = rms_norm(after_attn, moe_gain).astype(jnp.bfloat16)
    routes = expert_ids[0]
    top_k = routes.shape[1]
    experts = groups * lax.axis_size("exp")
    capacity = 3 * top_k * row_count // (2 * experts)
    maps = routing_maps(routes, expert_gates[0], experts, groups)
    made, weigh = serve(moe_in, maps, w_gate, w_up, w_down, capacity)
    result_rows = combine(made, weigh, after_attn)
    keys_out = append(cache_keys[0], fresh_keys, length)
    values_out = append(cache_values[0], fresh_values, length)
    return (result_rows[None], keys_out[None], values_out[None])


def solution(mesh):
    placed = (
        P("exp", None, None),
        P("exp", None, "req"),
        P("exp", None, "req"),
        P("exp"),
        P(),
        P("exp", "req"),
        P("exp", "req"),
        P("exp", "req"),
        P(),
        P(),
        P(("req", "exp"), None),
        P(),
        P("exp", "req", None),
        P("exp", "req", None),
        P(("req", "exp"), None, None),
        P(("req", "exp"), None, None),
        P(("req", "exp"), None, None),
    )
    return jax.shard_map(
        body,
        mesh=mesh,
        in_specs=placed,
        out_specs=(P("exp", "req", None), P("exp", None, "req"), P("exp", None, "req")),
        check_vma=False,
    )
```

```python
import functools
import math

import jax
import jax.numpy as jnp
from jax import lax
from jax.experimental import pallas as pl
from jax.experimental.pallas import tpu as pltpu
from jax.sharding import PartitionSpec as P

EPS = 1e-06
THETA = 1000000.0


MESH_ID = pl.DeviceIdType.MESH
CHUNKS = ((4, True, 0), (4, True, 1), (4, False, 0), (4, False, 1))
COUNT = len(CHUNKS)
EARLY = COUNT // 2
BACKWARD = (2, 3, 0, 1)


def spans(width):
    unit = width // sum(chunk[0] for chunk in CHUNKS)
    start = 0
    for share, planes_first, part in CHUNKS:
        yield start, share * unit, planes_first, part
        start += share * unit


def place():
    group = lax.axis_index("exp")
    return lax.axis_index("req"), group // 8, (group // 2) % 4, group % 2


def ring_peer(part, step, where):
    plane, row, column, core = where
    if part == 0:
        spot = (row + step) % 4
        return (plane, spot * 8 + column * 2 + core), spot
    spot = (column + step) % 4
    return (plane, row * 8 + spot * 2 + core), spot


def swap_peer(part, step, where):
    plane, row, column, core = where
    side = (core + step) % 2
    if part == 0:
        spot = (column + step // 2) % 4
        return (plane, row * 8 + spot * 2 + side), spot * 2 + side
    spot = (row + step // 2) % 4
    return (plane, spot * 8 + column * 2 + side), spot * 2 + side


def plane_peer(step, where):
    plane, row, column, core = where
    spot = (plane + step) % 4
    return (spot, row * 8 + column * 2 + core), spot


def greet(where):
    barrier = pltpu.get_barrier_semaphore()
    peers = [plane_peer(step, where)[0] for step in (1, 2, 3)]
    peers += [swap_peer(0, step, where)[0] for step in range(1, 8)]
    peers += [swap_peer(1, step, where)[0] for step in range(2, 8)]
    for peer in peers:
        pl.semaphore_signal(barrier, inc=1, device_id=peer, device_id_type=MESH_ID)
    pl.semaphore_wait(barrier, len(peers))


def remote(src, dst, send_sem, recv_sem, peer):
    return pltpu.make_async_remote_copy(
        src_ref=src,
        dst_ref=dst,
        send_sem=send_sem,
        recv_sem=recv_sem,
        device_id=peer,
        device_id_type=MESH_ID,
    )


def hops(planes_first, part, place_at, where):
    along_planes = lambda step: plane_peer(step, where)
    along_ring = lambda step: ring_peer(part, step, where)
    first = (along_planes, where[0]) if planes_first else (along_ring, place_at[part])
    second = (along_ring, place_at[part]) if planes_first else (along_planes, where[0])
    return first, second


def serve_body(
    rows_ref, map_ref, gate_ref, up_ref, down_ref, made_ref, weigh_ref,
    tokens, maps, pick, outbox, inbox, w_gate, w_up, w_down, partial, made,
    f_send, f_recv, b_send, b_recv, c_send, c_recv, m_send, m_recv, n_send, n_recv,
    local_sem, w_sem, made_sem,
):
    where = place()
    plane, row, column, core = where
    at = (row, column)
    chunks = tuple(spans(rows_ref.shape[1]))
    loads = [
        pltpu.make_async_copy(src.at[0], dst, w_sem.at[i])
        for i, (src, dst) in enumerate(((gate_ref, w_gate), (up_ref, w_up), (down_ref, w_down)))
    ]
    for load in loads:
        load.start()
    for part in range(2):
        maps[part, at[part], plane] = map_ref[plane]
    for q, (start, size, planes_first, part) in enumerate(chunks):
        tokens[q][at[part], plane] = rows_ref[:, start : start + size]
    greet(where)
    sent = []

    def send(copy):
        copy.start()
        sent.append(copy)

    for part in range(2):
        for step in (1, 2, 3):
            peer, spot = plane_peer(step, where)
            send(remote(
                map_ref.at[spot], maps.at[part, at[part], plane],
                m_send.at[part, step], m_recv.at[part, plane], peer,
            ))
    for q, (start, size, planes_first, part) in enumerate(chunks):
        (first, here), _ = hops(planes_first, part, at, where)
        for step in (1, 2, 3):
            peer, spot = first(step)
            send(remote(
                rows_ref.at[:, start : start + size], tokens[q].at[at[part], plane],
                f_send.at[q, step], f_recv.at[q, here], peer,
            ))
    for part in range(2):
        for step in (1, 2, 3):
            peer, spot = plane_peer(step, where)
            slot = maps.at[part, at[part], spot]
            remote(slot, slot, m_send.at[part, step], m_recv.at[part, spot], peer).wait_recv()
        for step in (1, 2, 3):
            peer, spot = ring_peer(part, step, where)
            slot = maps.at[part, at[part]]
            send(remote(slot, slot, n_send.at[part, step], n_recv.at[part, at[part]], peer))
    for q, (start, size, planes_first, part) in enumerate(chunks):
        (first, _), (second, here) = hops(planes_first, part, at, where)
        for step in (1, 2, 3):
            peer, spot = first(step)
            slot = tokens[q].at[at[part], spot] if planes_first else tokens[q].at[spot, plane]
            remote(slot, slot, f_send.at[q, step], f_recv.at[q, spot], peer).wait_recv()
        for step in (1, 2, 3):
            peer, spot = second(step)
            slot = tokens[q].at[at[part]] if planes_first else tokens[q].at[:, plane]
            send(remote(slot, slot, b_send.at[q, step], b_recv.at[q, here], peer))

    slots = pick.shape[2] // 32
    group = 4 * slots
    width = pick.shape[3]
    r_id = lax.broadcasted_iota(jnp.int32, (group, width), 0)
    c_id = lax.broadcasted_iota(jnp.int32, (group, width), 1)
    wanted = jnp.where(
        r_id // slots == c_id // (width // 4), (r_id % slots + 1).astype(jnp.float32), -1.0
    )
    for part in range(2):
        for step in (1, 2, 3):
            peer, spot = ring_peer(part, step, where)
            slot = maps.at[part, spot]
            remote(slot, slot, n_send.at[part, step], n_recv.at[part, spot], peer).wait_recv()

        def choose(b, carry, part=part):
            weighed = []
            for i in range(8):
                local = row * 8 + i if part == 0 else (i // 2) * 8 + column * 2 + i % 2
                named = jnp.concatenate(
                    [maps[part, b, z, pl.ds(local, 1), :] for z in range(4)], axis=1
                )
                gates = jnp.concatenate(
                    [maps[part, b, z, pl.ds(32 + local, 1), :] for z in range(4)], axis=1
                )
                hit = wanted == named
                pick[part, b, i * group : (i + 1) * group, :] = jnp.where(hit, 1.0, 0.0).astype(
                    jnp.bfloat16
                )
                weighed.append(jnp.where(hit, gates, 0.0))
            made_of = jnp.concatenate(weighed, axis=0)
            weigh_ref[part, b] = made_of.T.astype(jnp.bfloat16)
            return carry

        lax.fori_loop(0, 4, choose, 0)

    mine = (column * 2 + core, row * 2 + core)
    owns = []
    for q, (start, size, planes_first, part) in enumerate(chunks):
        _, (second, _) = hops(planes_first, part, at, where)
        for step in (1, 2, 3):
            peer, spot = second(step)
            slot = tokens[q].at[spot] if planes_first else tokens[q].at[:, spot]
            remote(slot, slot, b_send.at[q, step], b_recv.at[q, spot], peer).wait_recv()

        def gather(b, carry, q=q, part=part, size=size):
            rows = tokens[q][b].reshape(width, size)
            chosen = jnp.dot(pick[part, b], rows, preferred_element_type=jnp.float32)
            outbox[q][:, b] = chosen.astype(jnp.bfloat16).reshape(8, group, size)
            return carry

        lax.fori_loop(0, 4, gather, 0)
        cols = pl.ds(start, size)
        target = inbox.at[:, column, core, :, cols] if part == 0 else inbox.at[row, :, core, :, cols]
        for step in (2, 3, 4, 5, 6, 7, 1):
            peer, spot = swap_peer(part, step, where)
            send(remote(
                outbox[q].at[spot], target, c_send.at[q, step], c_recv.at[q, mine[part]], peer
            ))
        own = pltpu.make_async_copy(outbox[q].at[mine[part]], target, local_sem.at[q])
        own.start()
        owns.append(own)

    def arrive(which):
        for q in which:
            start, size, planes_first, part = chunks[q]
            cols = pl.ds(start, size)
            owns[q].wait()
            for step in range(1, 8):
                peer, spot = swap_peer(part, step, where)
                if part == 0:
                    slot = inbox.at[:, spot // 2, spot % 2, :, cols]
                else:
                    slot = inbox.at[spot // 2, :, spot % 2, :, cols]
                remote(
                    outbox[q].at[spot], slot, c_send.at[q, step], c_recv.at[q, spot], peer
                ).wait_recv()

    cut = chunks[EARLY][0]
    hidden_width = w_gate.shape[1]
    arrive(range(EARLY))
    for load in loads:
        load.wait()

    def begin(r, carry):
        x = inbox[r, :, :, :, 0:cut].reshape(8 * group, cut)
        partial[r, :, 0:hidden_width] = jnp.dot(
            x, w_gate[0:cut, :], preferred_element_type=jnp.float32
        )
        partial[r, :, hidden_width:] = jnp.dot(
            x, w_up[0:cut, :], preferred_element_type=jnp.float32
        )
        return carry

    lax.fori_loop(0, 4, begin, 0)
    arrive(range(EARLY, COUNT))

    def expert(r, carry):
        x = inbox[r, :, :, :, cut:].reshape(8 * group, inbox.shape[-1] - cut)
        gate = partial[r, :, 0:hidden_width] + jnp.dot(
            x, w_gate[cut:, :], preferred_element_type=jnp.float32
        )
        up = partial[r, :, hidden_width:] + jnp.dot(
            x, w_up[cut:, :], preferred_element_type=jnp.float32
        )
        hidden = (gate / (1.0 + jnp.exp(-gate)) * up).astype(jnp.bfloat16)
        out = jnp.dot(hidden, w_down[...], preferred_element_type=jnp.float32)

        @pl.when(r >= 2)
        def _():
            pltpu.make_async_copy(made.at[r % 2], made_ref.at[r - 2], made_sem.at[r % 2]).wait()

        made[r % 2] = out.astype(jnp.bfloat16).reshape(made.shape[1:])
        pltpu.make_async_copy(made.at[r % 2], made_ref.at[r], made_sem.at[r % 2]).start()
        return carry

    lax.fori_loop(0, 4, expert, 0)
    for r in (2, 3):
        pltpu.make_async_copy(made.at[r % 2], made_ref.at[r], made_sem.at[r % 2]).wait()
    for copy in sent:
        copy.wait_send()


def serve(rows, maps, w_gate, w_up, w_down, capacity):
    tokens, width = rows.shape
    hidden = w_gate.shape[2]
    sizes = [size for _, size, _, _ in spans(width)]
    group = 4 * capacity
    bf = jnp.bfloat16
    dma = pltpu.SemaphoreType.DMA
    vmem = pl.BlockSpec(memory_space=pltpu.VMEM)
    anywhere = pl.BlockSpec(memory_space=pl.ANY)
    return pl.pallas_call(
        serve_body,
        out_shape=(
            jax.ShapeDtypeStruct((4, 4, 2, group, width), bf),
            jax.ShapeDtypeStruct((2, 4, 4 * tokens, 8 * group), bf),
        ),
        in_specs=[vmem, vmem, anywhere, anywhere, anywhere],
        out_specs=(anywhere, vmem),
        scratch_shapes=[
            [pltpu.VMEM((4, 4, tokens, size), bf) for size in sizes],
            pltpu.VMEM((2, 4, 4) + maps.shape[1:], jnp.float32),
            pltpu.VMEM((2, 4, 8 * group, 4 * tokens), bf),
            [pltpu.VMEM((8, 4, group, size), bf) for size in sizes],
            pltpu.VMEM((4, 4, 2, group, width), bf),
            pltpu.VMEM((width, hidden), bf),
            pltpu.VMEM((width, hidden), bf),
            pltpu.VMEM((hidden, width), bf),
            pltpu.VMEM((4, 8 * group, 2 * hidden), jnp.float32),
            pltpu.VMEM((2, 4, 2, group, width), bf),
            dma((COUNT, 4)), dma((COUNT, 4)),
            dma((COUNT, 4)), dma((COUNT, 4)),
            dma((COUNT, 8)), dma((COUNT, 8)),
            dma((2, 4)), dma((2, 4)), dma((2, 4)), dma((2, 4)),
            dma((COUNT,)), dma((3,)), dma((2,)),
        ],
        compiler_params=pltpu.CompilerParams(
            collective_id=0, has_side_effects=True, vmem_limit_bytes=63 << 20
        ),
        name="serve",
    )(rows, maps, w_gate, w_up, w_down)


def combine_body(
    made_ref, weigh_ref, base_ref, out_ref,
    back, share, shares, total, totals,
    c_send, c_recv, b_send, b_recv, f_send, f_recv, local_sem,
):
    where = place()
    plane, row, column, core = where
    at = (row, column)
    mine = (column * 2 + core, row * 2 + core)
    tokens = base_ref.shape[0]
    forward = tuple(spans(base_ref.shape[1]))
    chunks = tuple((q, forward[q]) for q in BACKWARD)
    greet(where)
    sent = []

    def send(copy):
        copy.start()
        sent.append(copy)

    for q, (start, size, planes_first, part) in chunks:
        cols = pl.ds(start, size)

        def source(spot):
            if part == 0:
                return made_ref.at[:, spot // 2, spot % 2, :, cols]
            return made_ref.at[spot // 2, :, spot % 2, :, cols]

        for step in (2, 3, 4, 5, 6, 7, 1):
            peer, spot = swap_peer(part, step, where)
            send(remote(
                source(spot), back[q].at[:, mine[part]],
                c_send.at[q, step], c_recv.at[q, mine[part]], peer,
            ))
        pltpu.make_async_copy(
            source(mine[part]), back[q].at[:, mine[part]], local_sem.at[q]
        ).start()
    for q, (start, size, planes_first, part) in chunks:
        for step in range(1, 8):
            peer, spot = swap_peer(part, step, where)
            slot = back[q].at[:, spot]
            remote(slot, slot, c_send.at[q, step], c_recv.at[q, spot], peer).wait_recv()
        slot = back[q].at[:, mine[part]]
        pltpu.make_async_copy(slot, slot, local_sem.at[q]).wait()

        def weigh(b, carry, q=q, part=part, size=size):
            rows = back[q][b].reshape(weigh_ref.shape[-1], size)
            summed = jnp.dot(weigh_ref[part, b], rows, preferred_element_type=jnp.float32)
            share[q][b] = summed.astype(jnp.bfloat16).reshape(4, tokens, size)
            return carry

        lax.fori_loop(0, 4, weigh, 0)
        _, (second, here) = hops(planes_first, part, at, where)
        for step in (1, 2, 3):
            peer, spot = second(step)
            slot = share[q].at[spot] if planes_first else share[q].at[:, spot]
            send(remote(
                slot, shares[q].at[here], b_send.at[q, step], b_recv.at[q, here], peer
            ))
    for q, (start, size, planes_first, part) in chunks:
        (first, near), (second, here) = hops(planes_first, part, at, where)
        added = share[q][here] if planes_first else share[q][:, here]
        added = added.astype(jnp.float32)
        for step in (1, 2, 3):
            peer, spot = second(step)
            slot = shares[q].at[spot]
            remote(slot, slot, b_send.at[q, step], b_recv.at[q, spot], peer).wait_recv()
            added = added + shares[q][spot].astype(jnp.float32)
        total[q][...] = added.astype(jnp.bfloat16)
        for step in (1, 2, 3):
            peer, spot = first(step)
            send(remote(
                total[q].at[spot], totals[q].at[near],
                f_send.at[q, step], f_recv.at[q, near], peer,
            ))
    for q, (start, size, planes_first, part) in chunks:
        (first, near), _ = hops(planes_first, part, at, where)
        cols = slice(start, start + size)
        added = total[q][near].astype(jnp.float32)
        for step in (1, 2, 3):
            peer, spot = first(step)
            slot = totals[q].at[spot]
            remote(slot, slot, f_send.at[q, step], f_recv.at[q, spot], peer).wait_recv()
            added = added + totals[q][spot].astype(jnp.float32)
        out_ref[:, cols] = (base_ref[:, cols].astype(jnp.float32) + added).astype(jnp.bfloat16)
    for copy in sent:
        copy.wait_send()


def combine(made, weigh, base):
    tokens, width = base.shape
    sizes = [size for _, size, _, _ in spans(width)]
    group = made.shape[3]
    bf = jnp.bfloat16
    dma = pltpu.SemaphoreType.DMA
    vmem = pl.BlockSpec(memory_space=pltpu.VMEM)
    return pl.pallas_call(
        combine_body,
        out_shape=jax.ShapeDtypeStruct(base.shape, bf),
        in_specs=[pl.BlockSpec(memory_space=pl.ANY), vmem, vmem],
        out_specs=vmem,
        scratch_shapes=[
            [pltpu.VMEM((4, 8, group, size), bf) for size in sizes],
            [pltpu.VMEM((4, 4, tokens, size), bf) for size in sizes],
            [pltpu.VMEM((4, 4, tokens, size), bf) for size in sizes],
            [pltpu.VMEM((4, tokens, size), bf) for size in sizes],
            [pltpu.VMEM((4, tokens, size), bf) for size in sizes],
            dma((COUNT, 8)), dma((COUNT, 8)),
            dma((COUNT, 4)), dma((COUNT, 4)),
            dma((COUNT, 4)), dma((COUNT, 4)), dma((COUNT,)),
        ],
        compiler_params=pltpu.CompilerParams(
            collective_id=1, has_side_effects=True, vmem_limit_bytes=62 << 20
        ),
        name="combine",
    )(made, weigh, base)


def routing_maps(routes, gates, experts, planes):
    rows = routes.shape[0]
    ids = routes.T[None, :, :]
    hit = ids == jnp.arange(experts, dtype=jnp.int32)[:, None, None]
    named = jnp.sum(hit.astype(jnp.float32), axis=1)
    weight = jnp.sum(jnp.where(hit, gates.T[None, :, :], 0.0), axis=1)
    upto = (
        jnp.arange(rows, dtype=jnp.int32)[:, None] <= jnp.arange(rows, dtype=jnp.int32)[None, :]
    )
    order = jnp.dot(
        named.astype(jnp.bfloat16), upto.astype(jnp.bfloat16), preferred_element_type=jnp.float32
    )
    slot = order * named
    per_plane = experts // planes
    return jnp.concatenate(
        [slot.reshape(planes, per_plane, rows), weight.reshape(planes, per_plane, rows)], axis=1
    )


def front_body(
    exp_scale, length_ref, tokens_ref, gain_ref, wq_ref, wk_ref, wv_ref, cos_ref, sin_ref,
    q_gain_ref, k_gain_ref, ck_ref, cv_ref, wo_ref, moe_gain_ref,
    after_ref, moe_ref, fk_ref, fv_ref,
    weights, w_out, normed, proj, queries, kaug, vaug, attended, share, shares,
    s_send, s_recv, t_send, t_recv, x_send, x_recv, z_send, z_recv, cache_sem,
):
    where = place()
    plane, row, column, core = where
    stretch_len = tokens_ref.shape[0]
    width = q_gain_ref.shape[1]
    heads = queries.shape[0]
    cached = ck_ref.shape[1]
    fresh = fk_ref.shape[0]
    block = stretch_len // 4
    caches = [
        pltpu.make_async_copy(src.at[0], dst.at[0:cached, 0:width], cache_sem.at[i])
        for i, (src, dst) in enumerate(((ck_ref, kaug), (cv_ref, vaug)))
    ]
    for copy in caches:
        copy.start()
    q_cols = wq_ref.shape[1]
    k_cols = wk_ref.shape[1]
    weights[row, column, core, :, 0:q_cols] = wq_ref[...]
    weights[row, column, core, :, q_cols : q_cols + k_cols] = wk_ref[...]
    weights[row, column, core, :, q_cols + k_cols :] = wv_ref[...]
    w_out[row, column, core] = wo_ref[...]
    greet(where)
    sent = []

    def send(copy):
        copy.start()
        sent.append(copy)

    arrays = (weights, w_out)

    def half(array, part):
        middle = array.shape[-1] // 2
        return slice(0, middle) if part == 0 else slice(middle, 2 * middle)

    def near(n, part, spot_row, spot_column, side):
        return arrays[n].at[spot_row, spot_column, side, :, half(arrays[n], part)]

    def line(n, part, spot):
        if part == 0:
            return arrays[n].at[:, spot, core, :, half(arrays[n], part)]
        return arrays[n].at[spot, :, core, :, half(arrays[n], part)]

    at = (row, column)
    across = (column, row)
    for n in range(2):
        for part in range(2):
            for step in (1, 2, 3):
                peer, spot = ring_peer(part, step, where)
                slot = near(n, part, row, column, core)
                send(remote(
                    slot, slot, s_send.at[n, part, step], s_recv.at[n, part, at[part]], peer
                ))

    def second_stage(n):
        for part in range(2):
            for step in (1, 2, 3):
                peer, spot = ring_peer(part, step, where)
                slot = near(n, part, spot, column, core) if part == 0 else near(
                    n, part, row, spot, core
                )
                remote(
                    slot, slot, s_send.at[n, part, step], s_recv.at[n, part, spot], peer
                ).wait_recv()
            for step in (1, 2, 3):
                peer, spot = ring_peer(1 - part, step, where)
                slot = line(n, part, across[part])
                send(remote(
                    slot, slot, t_send.at[n, part, step], t_recv.at[n, part, across[part]], peer
                ))

    def hand_over(n):
        for part in range(2):
            for step in (1, 2, 3):
                peer, spot = ring_peer(1 - part, step, where)
                slot = line(n, part, spot)
                remote(
                    slot, slot, t_send.at[n, part, step], t_recv.at[n, part, spot], peer
                ).wait_recv()
            peer, _ = swap_peer(0, 1, where)
            slot = arrays[n].at[:, :, core, :, half(arrays[n], part)]
            pair(n, part).start()

    def pair(n, part):
        peer, _ = swap_peer(0, 1, where)
        slot = arrays[n].at[:, :, core, :, half(arrays[n], part)]
        return remote(slot, slot, x_send.at[n, part], x_recv.at[n, part], peer)

    def handed(n):
        for part in range(2):
            peer, _ = swap_peer(0, 1, where)
            slot = arrays[n].at[:, :, 1 - core, :, half(arrays[n], part)]
            remote(slot, slot, x_send.at[n, part], x_recv.at[n, part], peer).wait_recv()

    def normalize(i, carry):
        rows = pl.ds(i * block, block)
        values = tokens_ref[rows, :].astype(jnp.float32)
        factor = lax.rsqrt(jnp.mean(values * values, axis=-1, keepdims=True) + EPS)
        normed[rows, :] = (values * factor * gain_ref[...]).astype(jnp.bfloat16)
        return carry

    lax.fori_loop(0, 4, normalize, 0)
    second_stage(0)
    span = cached + fresh
    position = lax.broadcasted_iota(jnp.int32, (span, width), 0)
    lane = lax.broadcasted_iota(jnp.int32, (span, width), 1)
    hidden = (lane == 0) & (position >= length_ref[0]) & (position < cached)
    kaug[:, width:] = jnp.where(hidden, -1e30, 0.0).astype(jnp.bfloat16)
    vaug[:, width:] = jnp.ones((span, width), jnp.bfloat16)
    hand_over(0)
    second_stage(1)
    handed(0)

    def project(i, carry):
        rows = pl.ds(i * block, block)
        flat = weights[...].reshape(normed.shape[1], weights.shape[-1])
        proj[rows, :] = jnp.dot(normed[rows, :], flat, preferred_element_type=jnp.float32)
        return carry

    lax.fori_loop(0, 4, project, 0)

    def turned(values, gain):
        factor = lax.rsqrt(jnp.mean(values * values, axis=-1, keepdims=True) + EPS)
        values = values * factor * gain
        swapped = pltpu.roll(values, width // 2, 1)
        return (values * cos_ref[...] + swapped * sin_ref[...]).astype(jnp.bfloat16)

    for head in range(heads):
        queries[head] = turned(proj[:, head * width : (head + 1) * width], q_gain_ref[...])
    new_keys = turned(proj[:, q_cols : q_cols + k_cols], k_gain_ref[...])
    new_values = proj[:, q_cols + k_cols :].astype(jnp.bfloat16)
    fk_ref[...] = new_keys
    fv_ref[...] = new_values
    for copy in caches:
        copy.wait()
    kaug[cached:, 0:width] = new_keys
    vaug[cached:, 0:width] = new_values

    dims = (((1,), (1,)), ((), ()))
    count = heads * block

    def attend(spot):
        own = queries[:, pl.ds(spot * block, block), :].reshape(count, width)
        widened = jnp.concatenate([own, jnp.ones((count, width), jnp.bfloat16)], axis=1)
        old = lax.dot_general(widened, kaug[0:cached, :], dims, preferred_element_type=jnp.float32)
        new = lax.dot_general(
            own, kaug[cached:, 0:width], dims, preferred_element_type=jnp.float32
        )
        token = lax.broadcasted_iota(jnp.int32, (count, fresh), 0) % block + spot * block
        new = jnp.where(lax.broadcasted_iota(jnp.int32, (count, fresh), 1) <= token, new, -1e30)
        peak = jnp.maximum(
            jnp.max(old, axis=1, keepdims=True), jnp.max(new, axis=1, keepdims=True)
        )
        old = jnp.exp2((old - peak) * exp_scale).astype(jnp.bfloat16)
        new = jnp.exp2((new - peak) * exp_scale).astype(jnp.bfloat16)
        mixed = jnp.dot(old, vaug[0:cached, :], preferred_element_type=jnp.float32) + jnp.dot(
            new, vaug[cached:, :], preferred_element_type=jnp.float32
        )
        mixed = (mixed[:, :width] / mixed[:, width:]).astype(jnp.bfloat16)
        for head in range(heads):
            attended[spot, :, head * width : (head + 1) * width] = mixed[
                head * block : (head + 1) * block
            ]

    def project_out(spot):
        flat = w_out[...].reshape(attended.shape[2], w_out.shape[-1])
        return jnp.dot(attended[spot], flat, preferred_element_type=jnp.float32)

    def give(i):
        spot = (plane + 1 + i) % 4
        share[spot] = project_out(spot).astype(jnp.bfloat16)
        remote(
            share.at[spot], shares.at[plane], z_send.at[spot], z_recv.at[plane],
            (spot, row * 8 + column * 2 + core),
        ).start()

    def turn(i, carry):
        attend((plane + 1 + i) % 4)

        @pl.when(i == 0)
        def _():
            hand_over(1)

        @pl.when(i == 1)
        def _():
            handed(1)
            give(0)

        @pl.when((i > 0) & (i < 3))
        def _():
            give(i)

        return carry

    lax.fori_loop(0, 4, turn, 0)
    added = project_out(plane)
    for step in (1, 2, 3):
        peer, spot = plane_peer(step, where)
        remote(
            share.at[spot], shares.at[spot], z_send.at[spot], z_recv.at[spot], peer
        ).wait_recv()
        added = added + shares[spot].astype(jnp.float32)
    resident = tokens_ref[pl.ds(pl.multiple_of(plane * block, block), block), :]
    after = (resident.astype(jnp.float32) + added).astype(jnp.bfloat16)
    after_ref[...] = after
    values = after.astype(jnp.float32)
    factor = lax.rsqrt(jnp.mean(values * values, axis=-1, keepdims=True) + EPS)
    moe_ref[...] = (values * factor * moe_gain_ref[...]).astype(jnp.bfloat16)
    for copy in sent:
        copy.wait_send()
    for n in range(2):
        for part in range(2):
            pair(n, part).wait_send()
    for step in (1, 2, 3):
        peer, spot = plane_peer(step, where)
        remote(
            share.at[spot], shares.at[spot], z_send.at[spot], z_recv.at[spot], peer
        ).wait_send()


def front(
    length, tokens, attn_gain, w_query, w_key, w_value, cosine, sine, q_gain, k_gain,
    cache_keys, cache_values, w_out, moe_gain,
):
    stretch_len, model_width = tokens.shape
    width = q_gain.shape[0]
    heads = w_query.shape[1] // width
    columns = w_query.shape[1] + w_key.shape[1] + w_value.shape[1]
    span = cache_keys.shape[1] + stretch_len
    block = stretch_len // 4
    bf = jnp.bfloat16
    dma = pltpu.SemaphoreType.DMA
    vmem = pl.BlockSpec(memory_space=pltpu.VMEM)
    anywhere = pl.BlockSpec(memory_space=pl.ANY)
    return pl.pallas_call(
        functools.partial(front_body, width ** -0.5 * math.log2(math.e)),
        out_shape=(
            jax.ShapeDtypeStruct((block, model_width), bf),
            jax.ShapeDtypeStruct((block, model_width), bf),
            jax.ShapeDtypeStruct((stretch_len, width), bf),
            jax.ShapeDtypeStruct((stretch_len, width), bf),
        ),
        in_specs=[pl.BlockSpec(memory_space=pltpu.SMEM)] + [vmem] * 9 + [anywhere] * 2 + [vmem] * 2,
        out_specs=(vmem,) * 4,
        scratch_shapes=[
            pltpu.VMEM((4, 4, 2, w_query.shape[0], columns), bf),
            pltpu.VMEM((4, 4, 2, w_out.shape[0], model_width), bf),
            pltpu.VMEM((stretch_len, model_width), bf),
            pltpu.VMEM((stretch_len, columns), jnp.float32),
            pltpu.VMEM((heads, stretch_len, width), bf),
            pltpu.VMEM((span, 2 * width), bf),
            pltpu.VMEM((span, 2 * width), bf),
            pltpu.VMEM((4, block, heads * width), bf),
            pltpu.VMEM((4, block, model_width), bf),
            pltpu.VMEM((4, block, model_width), bf),
            dma((2, 2, 4)), dma((2, 2, 4)), dma((2, 2, 4)), dma((2, 2, 4)),
            dma((2, 2)), dma((2, 2)), dma((4,)), dma((4,)), dma((2,)),
        ],
        compiler_params=pltpu.CompilerParams(
            collective_id=2, has_side_effects=True, vmem_limit_bytes=63 << 20
        ),
        name="front",
    )(
        length, tokens, attn_gain[None], w_query, w_key, w_value, cosine, sine,
        q_gain[None], k_gain[None], cache_keys, cache_values, w_out, moe_gain[None],
    )


def turning(length, stretch_len, width):
    half_dim = width // 2
    frequency = THETA ** (-jnp.arange(half_dim, dtype=jnp.float32) * 2.0 / width)
    positions = length + jnp.arange(stretch_len, dtype=jnp.int32)
    angles = positions.astype(jnp.float32)[:, None] * frequency[None, :]
    cosine, sine = jnp.cos(angles), jnp.sin(angles)
    return jnp.concatenate([cosine, cosine], axis=1), jnp.concatenate([-sine, sine], axis=1)


def append(cache, fresh, length):
    span = cache.shape[0] + fresh.shape[0]
    padded = jnp.concatenate([cache, jnp.zeros_like(fresh)], axis=0)
    kept_rows = jnp.where(
        (jnp.arange(span, dtype=jnp.int32) < length)[:, None], padded, jnp.zeros_like(padded)
    )
    return lax.dynamic_update_slice(kept_rows, fresh, (length, jnp.zeros((), jnp.int32)))


def body(
    hidden_in,
    cache_keys,
    cache_values,
    cache_len,
    attn_gain,
    w_query,
    w_key,
    w_value,
    q_gain,
    k_gain,
    w_out,
    moe_gain,
    expert_ids,
    expert_gates,
    w_gate,
    w_up,
    w_down,
):
    tokens = hidden_in[0]
    stretch_len = tokens.shape[0]
    length = cache_len[0]
    groups = lax.axis_size("req")
    row_count = stretch_len // groups
    cosine, sine = turning(length, stretch_len, q_gain.shape[0])
    after_attn, moe_in, fresh_keys, fresh_values = front(
        cache_len, tokens, attn_gain, w_query, w_key, w_value, cosine, sine, q_gain, k_gain,
        cache_keys, cache_values, w_out, moe_gain,
    )
    routes = expert_ids[0]
    top_k = routes.shape[1]
    experts = groups * lax.axis_size("exp")
    capacity = 3 * top_k * row_count // (2 * experts)
    maps = routing_maps(routes, expert_gates[0], experts, groups)
    made, weigh = serve(moe_in, maps, w_gate, w_up, w_down, capacity)
    result_rows = combine(made, weigh, after_attn)
    keys_out = append(cache_keys[0], fresh_keys, length)
    values_out = append(cache_values[0], fresh_values, length)
    return (result_rows[None], keys_out[None], values_out[None])


def solution(mesh):
    placed = (
        P("exp", None, None),
        P("exp", None, "req"),
        P("exp", None, "req"),
        P("exp"),
        P(),
        P("exp", "req"),
        P("exp", "req"),
        P("exp", "req"),
        P(),
        P(),
        P(("req", "exp"), None),
        P(),
        P("exp", "req", None),
        P("exp", "req", None),
        P(("req", "exp"), None, None),
        P(("req", "exp"), None, None),
        P(("req", "exp"), None, None),
    )
    return jax.shard_map(
        body,
        mesh=mesh,
        in_specs=placed,
        out_specs=(P("exp", "req", None), P("exp", None, "req"), P("exp", None, "req")),
        check_vma=False,
    )
```

```python
import functools
import math

import jax
import jax.numpy as jnp
from jax import lax
from jax.experimental import pallas as pl
from jax.experimental.pallas import tpu as pltpu
from jax.sharding import PartitionSpec as P

EPS = 1e-06
THETA = 1000000.0


MESH_ID = pl.DeviceIdType.MESH
CHUNKS = ((4, True, 0), (4, True, 1), (4, False, 0), (4, False, 1))
COUNT = len(CHUNKS)
EARLY = COUNT // 2
BACKWARD = (2, 3, 0, 1)


def spans(width):
    unit = width // sum(chunk[0] for chunk in CHUNKS)
    start = 0
    for share, planes_first, part in CHUNKS:
        yield start, share * unit, planes_first, part
        start += share * unit


def place():
    group = lax.axis_index("exp")
    return lax.axis_index("req"), group // 8, (group // 2) % 4, group % 2


def ring_peer(part, step, where):
    plane, row, column, core = where
    if part == 0:
        spot = (row + step) % 4
        return (plane, spot * 8 + column * 2 + core), spot
    spot = (column + step) % 4
    return (plane, row * 8 + spot * 2 + core), spot


def swap_peer(part, step, where):
    plane, row, column, core = where
    side = (core + step) % 2
    if part == 0:
        spot = (column + step // 2) % 4
        return (plane, row * 8 + spot * 2 + side), spot * 2 + side
    spot = (row + step // 2) % 4
    return (plane, spot * 8 + column * 2 + side), spot * 2 + side


def plane_peer(step, where):
    plane, row, column, core = where
    spot = (plane + step) % 4
    return (spot, row * 8 + column * 2 + core), spot


def greet(where):
    barrier = pltpu.get_barrier_semaphore()
    peers = [plane_peer(step, where)[0] for step in (1, 2, 3)]
    peers += [swap_peer(0, step, where)[0] for step in range(1, 8)]
    peers += [swap_peer(1, step, where)[0] for step in range(2, 8)]
    for peer in peers:
        pl.semaphore_signal(barrier, inc=1, device_id=peer, device_id_type=MESH_ID)
    pl.semaphore_wait(barrier, len(peers))


def remote(src, dst, send_sem, recv_sem, peer):
    return pltpu.make_async_remote_copy(
        src_ref=src,
        dst_ref=dst,
        send_sem=send_sem,
        recv_sem=recv_sem,
        device_id=peer,
        device_id_type=MESH_ID,
    )


def hops(planes_first, part, place_at, where):
    along_planes = lambda step: plane_peer(step, where)
    along_ring = lambda step: ring_peer(part, step, where)
    first = (along_planes, where[0]) if planes_first else (along_ring, place_at[part])
    second = (along_ring, place_at[part]) if planes_first else (along_planes, where[0])
    return first, second


def serve_body(
    rows_ref, map_ref, gate_ref, up_ref, down_ref, made_ref, weigh_ref,
    tokens, maps, pick, outbox, inbox, w_gate, w_up, w_down, partial, made,
    f_send, f_recv, b_send, b_recv, c_send, c_recv, m_send, m_recv, n_send, n_recv,
    local_sem, w_sem, made_sem,
):
    where = place()
    plane, row, column, core = where
    at = (row, column)
    chunks = tuple(spans(rows_ref.shape[1]))
    loads = [
        pltpu.make_async_copy(src.at[0], dst, w_sem.at[i])
        for i, (src, dst) in enumerate(((gate_ref, w_gate), (up_ref, w_up), (down_ref, w_down)))
    ]
    for load in loads:
        load.start()
    for part in range(2):
        maps[part, at[part], plane] = map_ref[plane]
    for q, (start, size, planes_first, part) in enumerate(chunks):
        tokens[q][at[part], plane] = rows_ref[:, start : start + size]
    greet(where)
    sent = []

    def send(copy):
        copy.start()
        sent.append(copy)

    for part in range(2):
        for step in (1, 2, 3):
            peer, spot = plane_peer(step, where)
            send(remote(
                map_ref.at[spot], maps.at[part, at[part], plane],
                m_send.at[part, step], m_recv.at[part, plane], peer,
            ))
    for q, (start, size, planes_first, part) in enumerate(chunks):
        (first, here), _ = hops(planes_first, part, at, where)
        for step in (1, 2, 3):
            peer, spot = first(step)
            send(remote(
                rows_ref.at[:, start : start + size], tokens[q].at[at[part], plane],
                f_send.at[q, step], f_recv.at[q, here], peer,
            ))
    for part in range(2):
        for step in (1, 2, 3):
            peer, spot = plane_peer(step, where)
            slot = maps.at[part, at[part], spot]
            remote(slot, slot, m_send.at[part, step], m_recv.at[part, spot], peer).wait_recv()
        for step in (1, 2, 3):
            peer, spot = ring_peer(part, step, where)
            slot = maps.at[part, at[part]]
            send(remote(slot, slot, n_send.at[part, step], n_recv.at[part, at[part]], peer))
    for q, (start, size, planes_first, part) in enumerate(chunks):
        (first, _), (second, here) = hops(planes_first, part, at, where)
        for step in (1, 2, 3):
            peer, spot = first(step)
            slot = tokens[q].at[at[part], spot] if planes_first else tokens[q].at[spot, plane]
            remote(slot, slot, f_send.at[q, step], f_recv.at[q, spot], peer).wait_recv()
        for step in (1, 2, 3):
            peer, spot = second(step)
            slot = tokens[q].at[at[part]] if planes_first else tokens[q].at[:, plane]
            send(remote(slot, slot, b_send.at[q, step], b_recv.at[q, here], peer))

    slots = pick.shape[2] // 32
    group = 4 * slots
    width = pick.shape[3]
    r_id = lax.broadcasted_iota(jnp.int32, (group, width), 0)
    c_id = lax.broadcasted_iota(jnp.int32, (group, width), 1)
    wanted = jnp.where(
        r_id // slots == c_id // (width // 4), (r_id % slots + 1).astype(jnp.float32), -1.0
    )
    for part in range(2):
        for step in (1, 2, 3):
            peer, spot = ring_peer(part, step, where)
            slot = maps.at[part, spot]
            remote(slot, slot, n_send.at[part, step], n_recv.at[part, spot], peer).wait_recv()

        def choose(b, carry, part=part):
            weighed = []
            for i in range(8):
                local = row * 8 + i if part == 0 else (i // 2) * 8 + column * 2 + i % 2
                named = jnp.concatenate(
                    [maps[part, b, z, pl.ds(local, 1), :] for z in range(4)], axis=1
                )
                gates = jnp.concatenate(
                    [maps[part, b, z, pl.ds(32 + local, 1), :] for z in range(4)], axis=1
                )
                hit = wanted == named
                pick[part, b, i * group : (i + 1) * group, :] = jnp.where(hit, 1.0, 0.0).astype(
                    jnp.bfloat16
                )
                weighed.append(jnp.where(hit, gates, 0.0))
            made_of = jnp.concatenate(weighed, axis=0)
            weigh_ref[part, b] = made_of.T.astype(jnp.bfloat16)
            return carry

        lax.fori_loop(0, 4, choose, 0)

    mine = (column * 2 + core, row * 2 + core)
    owns = []
    for q, (start, size, planes_first, part) in enumerate(chunks):
        _, (second, _) = hops(planes_first, part, at, where)
        for step in (1, 2, 3):
            peer, spot = second(step)
            slot = tokens[q].at[spot] if planes_first else tokens[q].at[:, spot]
            remote(slot, slot, b_send.at[q, step], b_recv.at[q, spot], peer).wait_recv()

        def gather(b, carry, q=q, part=part, size=size):
            rows = tokens[q][b].reshape(width, size)
            chosen = jnp.dot(pick[part, b], rows, preferred_element_type=jnp.float32)
            outbox[q][:, b] = chosen.astype(jnp.bfloat16).reshape(8, group, size)
            return carry

        lax.fori_loop(0, 4, gather, 0)
        cols = pl.ds(start, size)
        target = inbox.at[:, column, core, :, cols] if part == 0 else inbox.at[row, :, core, :, cols]
        for step in (2, 3, 4, 5, 6, 7, 1):
            peer, spot = swap_peer(part, step, where)
            send(remote(
                outbox[q].at[spot], target, c_send.at[q, step], c_recv.at[q, mine[part]], peer
            ))
        own = pltpu.make_async_copy(outbox[q].at[mine[part]], target, local_sem.at[q])
        own.start()
        owns.append(own)

    def arrive(which):
        for q in which:
            start, size, planes_first, part = chunks[q]
            cols = pl.ds(start, size)
            owns[q].wait()
            for step in range(1, 8):
                peer, spot = swap_peer(part, step, where)
                if part == 0:
                    slot = inbox.at[:, spot // 2, spot % 2, :, cols]
                else:
                    slot = inbox.at[spot // 2, :, spot % 2, :, cols]
                remote(
                    outbox[q].at[spot], slot, c_send.at[q, step], c_recv.at[q, spot], peer
                ).wait_recv()

    cut = chunks[EARLY][0]
    hidden_width = w_gate.shape[1]
    arrive(range(EARLY))
    for load in loads:
        load.wait()

    def begin(r, carry):
        x = inbox[r, :, :, :, 0:cut].reshape(8 * group, cut)
        partial[r, :, 0:hidden_width] = jnp.dot(
            x, w_gate[0:cut, :], preferred_element_type=jnp.float32
        )
        partial[r, :, hidden_width:] = jnp.dot(
            x, w_up[0:cut, :], preferred_element_type=jnp.float32
        )
        return carry

    lax.fori_loop(0, 4, begin, 0)
    arrive(range(EARLY, COUNT))

    def expert(r, carry):
        x = inbox[r, :, :, :, cut:].reshape(8 * group, inbox.shape[-1] - cut)
        gate = partial[r, :, 0:hidden_width] + jnp.dot(
            x, w_gate[cut:, :], preferred_element_type=jnp.float32
        )
        up = partial[r, :, hidden_width:] + jnp.dot(
            x, w_up[cut:, :], preferred_element_type=jnp.float32
        )
        hidden = (gate / (1.0 + jnp.exp(-gate)) * up).astype(jnp.bfloat16)
        out = jnp.dot(hidden, w_down[...], preferred_element_type=jnp.float32)

        @pl.when(r >= 2)
        def _():
            pltpu.make_async_copy(made.at[r % 2], made_ref.at[r - 2], made_sem.at[r % 2]).wait()

        made[r % 2] = out.astype(jnp.bfloat16).reshape(made.shape[1:])
        pltpu.make_async_copy(made.at[r % 2], made_ref.at[r], made_sem.at[r % 2]).start()
        return carry

    lax.fori_loop(0, 4, expert, 0)
    for r in (2, 3):
        pltpu.make_async_copy(made.at[r % 2], made_ref.at[r], made_sem.at[r % 2]).wait()
    for copy in sent:
        copy.wait_send()


def serve(rows, maps, w_gate, w_up, w_down, capacity):
    tokens, width = rows.shape
    hidden = w_gate.shape[2]
    sizes = [size for _, size, _, _ in spans(width)]
    group = 4 * capacity
    bf = jnp.bfloat16
    dma = pltpu.SemaphoreType.DMA
    vmem = pl.BlockSpec(memory_space=pltpu.VMEM)
    anywhere = pl.BlockSpec(memory_space=pl.ANY)
    return pl.pallas_call(
        serve_body,
        out_shape=(
            jax.ShapeDtypeStruct((4, 4, 2, group, width), bf),
            jax.ShapeDtypeStruct((2, 4, 4 * tokens, 8 * group), bf),
        ),
        in_specs=[vmem, vmem, anywhere, anywhere, anywhere],
        out_specs=(anywhere, vmem),
        scratch_shapes=[
            [pltpu.VMEM((4, 4, tokens, size), bf) for size in sizes],
            pltpu.VMEM((2, 4, 4) + maps.shape[1:], jnp.float32),
            pltpu.VMEM((2, 4, 8 * group, 4 * tokens), bf),
            [pltpu.VMEM((8, 4, group, size), bf) for size in sizes],
            pltpu.VMEM((4, 4, 2, group, width), bf),
            pltpu.VMEM((width, hidden), bf),
            pltpu.VMEM((width, hidden), bf),
            pltpu.VMEM((hidden, width), bf),
            pltpu.VMEM((4, 8 * group, 2 * hidden), jnp.float32),
            pltpu.VMEM((2, 4, 2, group, width), bf),
            dma((COUNT, 4)), dma((COUNT, 4)),
            dma((COUNT, 4)), dma((COUNT, 4)),
            dma((COUNT, 8)), dma((COUNT, 8)),
            dma((2, 4)), dma((2, 4)), dma((2, 4)), dma((2, 4)),
            dma((COUNT,)), dma((3,)), dma((2,)),
        ],
        compiler_params=pltpu.CompilerParams(
            collective_id=0, has_side_effects=True, vmem_limit_bytes=63 << 20
        ),
        name="serve",
    )(rows, maps, w_gate, w_up, w_down)


def combine_body(
    made_ref, weigh_ref, base_ref, out_ref,
    back, share, shares, total, totals,
    c_send, c_recv, b_send, b_recv, f_send, f_recv, local_sem,
):
    where = place()
    plane, row, column, core = where
    at = (row, column)
    mine = (column * 2 + core, row * 2 + core)
    tokens = base_ref.shape[0]
    forward = tuple(spans(base_ref.shape[1]))
    chunks = tuple((q, forward[q]) for q in BACKWARD)
    greet(where)
    sent = []

    def send(copy):
        copy.start()
        sent.append(copy)

    for q, (start, size, planes_first, part) in chunks:
        cols = pl.ds(start, size)

        def source(spot):
            if part == 0:
                return made_ref.at[:, spot // 2, spot % 2, :, cols]
            return made_ref.at[spot // 2, :, spot % 2, :, cols]

        for step in (2, 3, 4, 5, 6, 7, 1):
            peer, spot = swap_peer(part, step, where)
            send(remote(
                source(spot), back[q].at[:, mine[part]],
                c_send.at[q, step], c_recv.at[q, mine[part]], peer,
            ))
        pltpu.make_async_copy(
            source(mine[part]), back[q].at[:, mine[part]], local_sem.at[q]
        ).start()
    for q, (start, size, planes_first, part) in chunks:
        for step in range(1, 8):
            peer, spot = swap_peer(part, step, where)
            slot = back[q].at[:, spot]
            remote(slot, slot, c_send.at[q, step], c_recv.at[q, spot], peer).wait_recv()
        slot = back[q].at[:, mine[part]]
        pltpu.make_async_copy(slot, slot, local_sem.at[q]).wait()

        def weigh(b, carry, q=q, part=part, size=size):
            rows = back[q][b].reshape(weigh_ref.shape[-1], size)
            summed = jnp.dot(weigh_ref[part, b], rows, preferred_element_type=jnp.float32)
            share[q][b] = summed.astype(jnp.bfloat16).reshape(4, tokens, size)
            return carry

        lax.fori_loop(0, 4, weigh, 0)
        _, (second, here) = hops(planes_first, part, at, where)
        for step in (1, 2, 3):
            peer, spot = second(step)
            slot = share[q].at[spot] if planes_first else share[q].at[:, spot]
            send(remote(
                slot, shares[q].at[here], b_send.at[q, step], b_recv.at[q, here], peer
            ))
    for q, (start, size, planes_first, part) in chunks:
        (first, near), (second, here) = hops(planes_first, part, at, where)
        added = share[q][here] if planes_first else share[q][:, here]
        added = added.astype(jnp.float32)
        for step in (1, 2, 3):
            peer, spot = second(step)
            slot = shares[q].at[spot]
            remote(slot, slot, b_send.at[q, step], b_recv.at[q, spot], peer).wait_recv()
            added = added + shares[q][spot].astype(jnp.float32)
        total[q][...] = added.astype(jnp.bfloat16)
        for step in (1, 2, 3):
            peer, spot = first(step)
            send(remote(
                total[q].at[spot], totals[q].at[near],
                f_send.at[q, step], f_recv.at[q, near], peer,
            ))
    for q, (start, size, planes_first, part) in chunks:
        (first, near), _ = hops(planes_first, part, at, where)
        cols = slice(start, start + size)
        added = total[q][near].astype(jnp.float32)
        for step in (1, 2, 3):
            peer, spot = first(step)
            slot = totals[q].at[spot]
            remote(slot, slot, f_send.at[q, step], f_recv.at[q, spot], peer).wait_recv()
            added = added + totals[q][spot].astype(jnp.float32)
        out_ref[:, cols] = (base_ref[:, cols].astype(jnp.float32) + added).astype(jnp.bfloat16)
    for copy in sent:
        copy.wait_send()


def combine(made, weigh, base):
    tokens, width = base.shape
    sizes = [size for _, size, _, _ in spans(width)]
    group = made.shape[3]
    bf = jnp.bfloat16
    dma = pltpu.SemaphoreType.DMA
    vmem = pl.BlockSpec(memory_space=pltpu.VMEM)
    return pl.pallas_call(
        combine_body,
        out_shape=jax.ShapeDtypeStruct(base.shape, bf),
        in_specs=[pl.BlockSpec(memory_space=pl.ANY), vmem, vmem],
        out_specs=vmem,
        scratch_shapes=[
            [pltpu.VMEM((4, 8, group, size), bf) for size in sizes],
            [pltpu.VMEM((4, 4, tokens, size), bf) for size in sizes],
            [pltpu.VMEM((4, 4, tokens, size), bf) for size in sizes],
            [pltpu.VMEM((4, tokens, size), bf) for size in sizes],
            [pltpu.VMEM((4, tokens, size), bf) for size in sizes],
            dma((COUNT, 8)), dma((COUNT, 8)),
            dma((COUNT, 4)), dma((COUNT, 4)),
            dma((COUNT, 4)), dma((COUNT, 4)), dma((COUNT,)),
        ],
        compiler_params=pltpu.CompilerParams(
            collective_id=1, has_side_effects=True, vmem_limit_bytes=62 << 20
        ),
        name="combine",
    )(made, weigh, base)


def routing_maps(routes, gates, experts, planes):
    rows = routes.shape[0]
    ids = routes.T[None, :, :]
    hit = ids == jnp.arange(experts, dtype=jnp.int32)[:, None, None]
    named = jnp.sum(hit.astype(jnp.float32), axis=1)
    weight = jnp.sum(jnp.where(hit, gates.T[None, :, :], 0.0), axis=1)
    upto = (
        jnp.arange(rows, dtype=jnp.int32)[:, None] <= jnp.arange(rows, dtype=jnp.int32)[None, :]
    )
    order = jnp.dot(
        named.astype(jnp.bfloat16), upto.astype(jnp.bfloat16), preferred_element_type=jnp.float32
    )
    slot = order * named
    per_plane = experts // planes
    return jnp.concatenate(
        [slot.reshape(planes, per_plane, rows), weight.reshape(planes, per_plane, rows)], axis=1
    )


def front_body(
    exp_scale, length_ref, tokens_ref, gain_ref, wq_ref, wk_ref, wv_ref, cos_ref, sin_ref,
    q_gain_ref, k_gain_ref, ck_ref, cv_ref, wo_ref, moe_gain_ref,
    after_ref, moe_ref, fk_ref, fv_ref,
    weights, w_out, normed, proj, queries, kaug, vaug, attended, share, shares,
    s_send, s_recv, t_send, t_recv, x_send, x_recv, z_send, z_recv, cache_sem,
):
    where = place()
    plane, row, column, core = where
    stretch_len = tokens_ref.shape[0]
    width = q_gain_ref.shape[1]
    heads = queries.shape[0]
    cached = ck_ref.shape[1]
    fresh = fk_ref.shape[0]
    block = stretch_len // 4
    caches = [
        pltpu.make_async_copy(src.at[0], dst.at[0:cached, 0:width], cache_sem.at[i])
        for i, (src, dst) in enumerate(((ck_ref, kaug), (cv_ref, vaug)))
    ]
    for copy in caches:
        copy.start()
    q_cols = wq_ref.shape[1]
    k_cols = wk_ref.shape[1]
    weights[row, column, core, :, 0:q_cols] = wq_ref[...]
    weights[row, column, core, :, q_cols : q_cols + k_cols] = wk_ref[...]
    weights[row, column, core, :, q_cols + k_cols :] = wv_ref[...]
    w_out[row, column, core] = wo_ref[...]
    greet(where)
    sent = []

    def send(copy):
        copy.start()
        sent.append(copy)

    arrays = (weights, w_out)

    def half(array, part):
        middle = array.shape[-1] // 2
        return slice(0, middle) if part == 0 else slice(middle, 2 * middle)

    def near(n, part, spot_row, spot_column, side):
        return arrays[n].at[spot_row, spot_column, side, :, half(arrays[n], part)]

    def line(n, part, spot):
        if part == 0:
            return arrays[n].at[:, spot, core, :, half(arrays[n], part)]
        return arrays[n].at[spot, :, core, :, half(arrays[n], part)]

    at = (row, column)
    across = (column, row)
    for n in range(2):
        for part in range(2):
            for step in (1, 2, 3):
                peer, spot = ring_peer(part, step, where)
                slot = near(n, part, row, column, core)
                send(remote(
                    slot, slot, s_send.at[n, part, step], s_recv.at[n, part, at[part]], peer
                ))

    def second_stage(n):
        for part in range(2):
            for step in (1, 2, 3):
                peer, spot = ring_peer(part, step, where)
                slot = near(n, part, spot, column, core) if part == 0 else near(
                    n, part, row, spot, core
                )
                remote(
                    slot, slot, s_send.at[n, part, step], s_recv.at[n, part, spot], peer
                ).wait_recv()
            for step in (1, 2, 3):
                peer, spot = ring_peer(1 - part, step, where)
                slot = line(n, part, across[part])
                send(remote(
                    slot, slot, t_send.at[n, part, step], t_recv.at[n, part, across[part]], peer
                ))

    def hand_over(n):
        for part in range(2):
            for step in (1, 2, 3):
                peer, spot = ring_peer(1 - part, step, where)
                slot = line(n, part, spot)
                remote(
                    slot, slot, t_send.at[n, part, step], t_recv.at[n, part, spot], peer
                ).wait_recv()
            peer, _ = swap_peer(0, 1, where)
            slot = arrays[n].at[:, :, core, :, half(arrays[n], part)]
            pair(n, part).start()

    def pair(n, part):
        peer, _ = swap_peer(0, 1, where)
        slot = arrays[n].at[:, :, core, :, half(arrays[n], part)]
        return remote(slot, slot, x_send.at[n, part], x_recv.at[n, part], peer)

    def handed(n):
        for part in range(2):
            peer, _ = swap_peer(0, 1, where)
            slot = arrays[n].at[:, :, 1 - core, :, half(arrays[n], part)]
            remote(slot, slot, x_send.at[n, part], x_recv.at[n, part], peer).wait_recv()

    def normalize(i, carry):
        rows = pl.ds(i * block, block)
        values = tokens_ref[rows, :].astype(jnp.float32)
        factor = lax.rsqrt(jnp.mean(values * values, axis=-1, keepdims=True) + EPS)
        normed[rows, :] = (values * factor * gain_ref[...]).astype(jnp.bfloat16)
        return carry

    lax.fori_loop(0, 4, normalize, 0)
    second_stage(0)
    span = cached + fresh
    position = lax.broadcasted_iota(jnp.int32, (span, width), 0)
    lane = lax.broadcasted_iota(jnp.int32, (span, width), 1)
    hidden = (lane == 0) & (position >= length_ref[0]) & (position < cached)
    kaug[:, width:] = jnp.where(hidden, -1e30, 0.0).astype(jnp.bfloat16)
    vaug[:, width:] = jnp.ones((span, width), jnp.bfloat16)
    hand_over(0)
    second_stage(1)
    handed(0)

    def project(i, carry):
        rows = pl.ds(i * block, block)
        flat = weights[...].reshape(normed.shape[1], weights.shape[-1])
        proj[rows, :] = jnp.dot(normed[rows, :], flat, preferred_element_type=jnp.float32)
        return carry

    lax.fori_loop(0, 4, project, 0)

    def turned(values, gain):
        factor = lax.rsqrt(jnp.mean(values * values, axis=-1, keepdims=True) + EPS)
        values = values * factor * gain
        swapped = pltpu.roll(values, width // 2, 1)
        return (values * cos_ref[...] + swapped * sin_ref[...]).astype(jnp.bfloat16)

    for head in range(heads):
        queries[head] = turned(proj[:, head * width : (head + 1) * width], q_gain_ref[...])
    new_keys = turned(proj[:, q_cols : q_cols + k_cols], k_gain_ref[...])
    new_values = proj[:, q_cols + k_cols :].astype(jnp.bfloat16)
    fk_ref[...] = new_keys
    fv_ref[...] = new_values
    for copy in caches:
        copy.wait()
    kaug[cached:, 0:width] = new_keys
    vaug[cached:, 0:width] = new_values

    dims = (((1,), (1,)), ((), ()))
    count = heads * block

    def attend(spot):
        own = queries[:, pl.ds(spot * block, block), :].reshape(count, width)
        widened = jnp.concatenate([own, jnp.ones((count, width), jnp.bfloat16)], axis=1)
        old = lax.dot_general(widened, kaug[0:cached, :], dims, preferred_element_type=jnp.float32)
        new = lax.dot_general(
            own, kaug[cached:, 0:width], dims, preferred_element_type=jnp.float32
        )
        token = lax.broadcasted_iota(jnp.int32, (count, fresh), 0) % block + spot * block
        new = jnp.where(lax.broadcasted_iota(jnp.int32, (count, fresh), 1) <= token, new, -1e30)
        peak = jnp.maximum(
            jnp.max(old, axis=1, keepdims=True), jnp.max(new, axis=1, keepdims=True)
        )
        old = jnp.exp2((old - peak) * exp_scale).astype(jnp.bfloat16)
        new = jnp.exp2((new - peak) * exp_scale).astype(jnp.bfloat16)
        mixed = jnp.dot(old, vaug[0:cached, :], preferred_element_type=jnp.float32) + jnp.dot(
            new, vaug[cached:, :], preferred_element_type=jnp.float32
        )
        mixed = (mixed[:, :width] / mixed[:, width:]).astype(jnp.bfloat16)
        for head in range(heads):
            attended[spot, :, head * width : (head + 1) * width] = mixed[
                head * block : (head + 1) * block
            ]

    def project_out(spot):
        flat = w_out[...].reshape(attended.shape[2], w_out.shape[-1])
        return jnp.dot(attended[spot], flat, preferred_element_type=jnp.float32)

    def give(i):
        spot = (plane + 1 + i) % 4
        share[spot] = project_out(spot).astype(jnp.bfloat16)
        remote(
            share.at[spot], shares.at[plane], z_send.at[spot], z_recv.at[plane],
            (spot, row * 8 + column * 2 + core),
        ).start()

    def turn(i, carry):
        attend((plane + 1 + i) % 4)

        @pl.when(i == 0)
        def _():
            hand_over(1)

        @pl.when(i == 1)
        def _():
            handed(1)
            give(0)

        @pl.when((i > 0) & (i < 3))
        def _():
            give(i)

        return carry

    lax.fori_loop(0, 4, turn, 0)
    added = project_out(plane)
    for step in (1, 2, 3):
        peer, spot = plane_peer(step, where)
        remote(
            share.at[spot], shares.at[spot], z_send.at[spot], z_recv.at[spot], peer
        ).wait_recv()
        added = added + shares[spot].astype(jnp.float32)
    resident = tokens_ref[pl.ds(pl.multiple_of(plane * block, block), block), :]
    after = (resident.astype(jnp.float32) + added).astype(jnp.bfloat16)
    after_ref[...] = after
    values = after.astype(jnp.float32)
    factor = lax.rsqrt(jnp.mean(values * values, axis=-1, keepdims=True) + EPS)
    moe_ref[...] = (values * factor * moe_gain_ref[...]).astype(jnp.bfloat16)
    for copy in sent:
        copy.wait_send()
    for n in range(2):
        for part in range(2):
            pair(n, part).wait_send()
    for step in (1, 2, 3):
        peer, spot = plane_peer(step, where)
        remote(
            share.at[spot], shares.at[spot], z_send.at[spot], z_recv.at[spot], peer
        ).wait_send()


def front(
    length, tokens, attn_gain, w_query, w_key, w_value, cosine, sine, q_gain, k_gain,
    cache_keys, cache_values, w_out, moe_gain,
):
    stretch_len, model_width = tokens.shape
    width = q_gain.shape[0]
    heads = w_query.shape[1] // width
    columns = w_query.shape[1] + w_key.shape[1] + w_value.shape[1]
    span = cache_keys.shape[1] + stretch_len
    block = stretch_len // 4
    bf = jnp.bfloat16
    dma = pltpu.SemaphoreType.DMA
    vmem = pl.BlockSpec(memory_space=pltpu.VMEM)
    anywhere = pl.BlockSpec(memory_space=pl.ANY)
    return pl.pallas_call(
        functools.partial(front_body, width ** -0.5 * math.log2(math.e)),
        out_shape=(
            jax.ShapeDtypeStruct((block, model_width), bf),
            jax.ShapeDtypeStruct((block, model_width), bf),
            jax.ShapeDtypeStruct((stretch_len, width), bf),
            jax.ShapeDtypeStruct((stretch_len, width), bf),
        ),
        in_specs=[pl.BlockSpec(memory_space=pltpu.SMEM)] + [vmem] * 9 + [anywhere] * 2 + [vmem] * 2,
        out_specs=(vmem,) * 4,
        scratch_shapes=[
            pltpu.VMEM((4, 4, 2, w_query.shape[0], columns), bf),
            pltpu.VMEM((4, 4, 2, w_out.shape[0], model_width), bf),
            pltpu.VMEM((stretch_len, model_width), bf),
            pltpu.VMEM((stretch_len, columns), jnp.float32),
            pltpu.VMEM((heads, stretch_len, width), bf),
            pltpu.VMEM((span, 2 * width), bf),
            pltpu.VMEM((span, 2 * width), bf),
            pltpu.VMEM((4, block, heads * width), bf),
            pltpu.VMEM((4, block, model_width), bf),
            pltpu.VMEM((4, block, model_width), bf),
            dma((2, 2, 4)), dma((2, 2, 4)), dma((2, 2, 4)), dma((2, 2, 4)),
            dma((2, 2)), dma((2, 2)), dma((4,)), dma((4,)), dma((2,)),
        ],
        compiler_params=pltpu.CompilerParams(
            collective_id=2, has_side_effects=True, vmem_limit_bytes=63 << 20
        ),
        name="front",
    )(
        length, tokens, attn_gain[None], w_query, w_key, w_value, cosine, sine,
        q_gain[None], k_gain[None], cache_keys, cache_values, w_out, moe_gain[None],
    )


def turning(length, stretch_len, width):
    half_dim = width // 2
    frequency = THETA ** (-jnp.arange(half_dim, dtype=jnp.float32) * 2.0 / width)
    positions = length + jnp.arange(stretch_len, dtype=jnp.int32)
    angles = positions.astype(jnp.float32)[:, None] * frequency[None, :]
    cosine, sine = jnp.cos(angles), jnp.sin(angles)
    return jnp.concatenate([cosine, cosine], axis=1), jnp.concatenate([-sine, sine], axis=1)


def append_body(length_ref, ck_ref, cv_ref, fk_ref, fv_ref, ko_ref, vo_ref, moved):
    length = length_ref[0]
    cached = ck_ref.shape[1]
    fresh = fk_ref.shape[0]
    row = lax.broadcasted_iota(jnp.int32, ck_ref.shape[1:], 0)
    for cache, new, out in ((ck_ref, fk_ref, ko_ref), (cv_ref, fv_ref, vo_ref)):
        moved[...] = jnp.zeros_like(moved)
        moved[pl.ds(length, fresh), :] = new[...].astype(jnp.float32)
        tail = moved[...].astype(jnp.bfloat16)
        out[0, 0:cached] = jnp.where(row < length, cache[0], tail[0:cached])
        out[0, cached:] = tail[cached:]


def append(cache_keys, cache_values, fresh_keys, fresh_values, length):
    _, cached, width = cache_keys.shape
    span = cached + fresh_keys.shape[0]
    vmem = pl.BlockSpec(memory_space=pltpu.VMEM)
    return pl.pallas_call(
        append_body,
        out_shape=(jax.ShapeDtypeStruct((1, span, width), jnp.bfloat16),) * 2,
        in_specs=[pl.BlockSpec(memory_space=pltpu.SMEM)] + [vmem] * 4,
        out_specs=(vmem, vmem),
        scratch_shapes=[pltpu.VMEM((span, width), jnp.float32)],
        compiler_params=pltpu.CompilerParams(vmem_limit_bytes=32 << 20),
        name="append",
    )(length, cache_keys, cache_values, fresh_keys, fresh_values)


def body(
    hidden_in,
    cache_keys,
    cache_values,
    cache_len,
    attn_gain,
    w_query,
    w_key,
    w_value,
    q_gain,
    k_gain,
    w_out,
    moe_gain,
    expert_ids,
    expert_gates,
    w_gate,
    w_up,
    w_down,
):
    tokens = hidden_in[0]
    stretch_len = tokens.shape[0]
    length = cache_len[0]
    groups = lax.axis_size("req")
    row_count = stretch_len // groups
    cosine, sine = turning(length, stretch_len, q_gain.shape[0])
    after_attn, moe_in, fresh_keys, fresh_values = front(
        cache_len, tokens, attn_gain, w_query, w_key, w_value, cosine, sine, q_gain, k_gain,
        cache_keys, cache_values, w_out, moe_gain,
    )
    routes = expert_ids[0]
    top_k = routes.shape[1]
    experts = groups * lax.axis_size("exp")
    capacity = 3 * top_k * row_count // (2 * experts)
    maps = routing_maps(routes, expert_gates[0], experts, groups)
    made, weigh = serve(moe_in, maps, w_gate, w_up, w_down, capacity)
    result_rows = combine(made, weigh, after_attn)
    keys_out, values_out = append(
        cache_keys, cache_values, fresh_keys, fresh_values, cache_len
    )
    return (result_rows[None], keys_out, values_out)


def solution(mesh):
    placed = (
        P("exp", None, None),
        P("exp", None, "req"),
        P("exp", None, "req"),
        P("exp"),
        P(),
        P("exp", "req"),
        P("exp", "req"),
        P("exp", "req"),
        P(),
        P(),
        P(("req", "exp"), None),
        P(),
        P("exp", "req", None),
        P("exp", "req", None),
        P(("req", "exp"), None, None),
        P(("req", "exp"), None, None),
        P(("req", "exp"), None, None),
    )
    return jax.shard_map(
        body,
        mesh=mesh,
        in_specs=placed,
        out_specs=(P("exp", "req", None), P("exp", None, "req"), P("exp", None, "req")),
        check_vma=False,
    )
```

```python
import functools
import math

import jax
import jax.numpy as jnp
from jax import lax
from jax.experimental import pallas as pl
from jax.experimental.pallas import tpu as pltpu
from jax.sharding import PartitionSpec as P

EPS = 1e-06
THETA = 1000000.0


MESH_ID = pl.DeviceIdType.MESH
CHUNKS = ((4, True, 0), (4, True, 1), (4, False, 0), (4, False, 1))
COUNT = len(CHUNKS)
EARLY = COUNT // 2
BACKWARD = (2, 3, 0, 1)


def spans(width):
    unit = width // sum(chunk[0] for chunk in CHUNKS)
    start = 0
    for share, planes_first, part in CHUNKS:
        yield start, share * unit, planes_first, part
        start += share * unit


def place():
    group = lax.axis_index("exp")
    return lax.axis_index("req"), group // 8, (group // 2) % 4, group % 2


def ring_peer(part, step, where):
    plane, row, column, core = where
    if part == 0:
        spot = (row + step) % 4
        return (plane, spot * 8 + column * 2 + core), spot
    spot = (column + step) % 4
    return (plane, row * 8 + spot * 2 + core), spot


def swap_peer(part, step, where):
    plane, row, column, core = where
    side = (core + step) % 2
    if part == 0:
        spot = (column + step // 2) % 4
        return (plane, row * 8 + spot * 2 + side), spot * 2 + side
    spot = (row + step // 2) % 4
    return (plane, spot * 8 + column * 2 + side), spot * 2 + side


def plane_peer(step, where):
    plane, row, column, core = where
    spot = (plane + step) % 4
    return (spot, row * 8 + column * 2 + core), spot


def greet(where):
    barrier = pltpu.get_barrier_semaphore()
    peers = [plane_peer(step, where)[0] for step in (1, 2, 3)]
    peers += [swap_peer(0, step, where)[0] for step in range(1, 8)]
    peers += [swap_peer(1, step, where)[0] for step in range(2, 8)]
    for peer in peers:
        pl.semaphore_signal(barrier, inc=1, device_id=peer, device_id_type=MESH_ID)
    pl.semaphore_wait(barrier, len(peers))


def remote(src, dst, send_sem, recv_sem, peer):
    return pltpu.make_async_remote_copy(
        src_ref=src,
        dst_ref=dst,
        send_sem=send_sem,
        recv_sem=recv_sem,
        device_id=peer,
        device_id_type=MESH_ID,
    )


def hops(planes_first, part, place_at, where):
    along_planes = lambda step: plane_peer(step, where)
    along_ring = lambda step: ring_peer(part, step, where)
    first = (along_planes, where[0]) if planes_first else (along_ring, place_at[part])
    second = (along_ring, place_at[part]) if planes_first else (along_planes, where[0])
    return first, second


def serve_body(
    rows_ref, map_ref, gate_ref, up_ref, down_ref, made_ref, weigh_ref,
    tokens, maps, pick, outbox, inbox, w_gate, w_up, w_down, partial, made,
    f_send, f_recv, b_send, b_recv, c_send, c_recv, m_send, m_recv, n_send, n_recv,
    local_sem, w_sem, made_sem,
):
    where = place()
    plane, row, column, core = where
    at = (row, column)
    chunks = tuple(spans(rows_ref.shape[1]))
    loads = [
        pltpu.make_async_copy(src.at[0], dst, w_sem.at[i])
        for i, (src, dst) in enumerate(((gate_ref, w_gate), (up_ref, w_up), (down_ref, w_down)))
    ]
    for load in loads:
        load.start()
    for part in range(2):
        maps[part, at[part], plane] = map_ref[plane]
    for q, (start, size, planes_first, part) in enumerate(chunks):
        tokens[q][at[part], plane] = rows_ref[:, start : start + size]
    greet(where)
    sent = []

    def send(copy):
        copy.start()
        sent.append(copy)

    for part in range(2):
        for step in (1, 2, 3):
            peer, spot = plane_peer(step, where)
            send(remote(
                map_ref.at[spot], maps.at[part, at[part], plane],
                m_send.at[part, step], m_recv.at[part, plane], peer,
            ))
    for q, (start, size, planes_first, part) in enumerate(chunks):
        (first, here), _ = hops(planes_first, part, at, where)
        for step in (1, 2, 3):
            peer, spot = first(step)
            send(remote(
                rows_ref.at[:, start : start + size], tokens[q].at[at[part], plane],
                f_send.at[q, step], f_recv.at[q, here], peer,
            ))
    for part in range(2):
        for step in (1, 2, 3):
            peer, spot = plane_peer(step, where)
            slot = maps.at[part, at[part], spot]
            remote(slot, slot, m_send.at[part, step], m_recv.at[part, spot], peer).wait_recv()
        for step in (1, 2, 3):
            peer, spot = ring_peer(part, step, where)
            slot = maps.at[part, at[part]]
            send(remote(slot, slot, n_send.at[part, step], n_recv.at[part, at[part]], peer))
    for q, (start, size, planes_first, part) in enumerate(chunks):
        (first, _), (second, here) = hops(planes_first, part, at, where)
        for step in (1, 2, 3):
            peer, spot = first(step)
            slot = tokens[q].at[at[part], spot] if planes_first else tokens[q].at[spot, plane]
            remote(slot, slot, f_send.at[q, step], f_recv.at[q, spot], peer).wait_recv()
        for step in (1, 2, 3):
            peer, spot = second(step)
            slot = tokens[q].at[at[part]] if planes_first else tokens[q].at[:, plane]
            send(remote(slot, slot, b_send.at[q, step], b_recv.at[q, here], peer))

    slots = pick.shape[2] // 32
    group = 4 * slots
    width = pick.shape[3]
    r_id = lax.broadcasted_iota(jnp.int32, (group, width), 0)
    c_id = lax.broadcasted_iota(jnp.int32, (group, width), 1)
    wanted = jnp.where(
        r_id // slots == c_id // (width // 4), (r_id % slots + 1).astype(jnp.float32), -1.0
    )
    for part in range(2):
        for step in (1, 2, 3):
            peer, spot = ring_peer(part, step, where)
            slot = maps.at[part, spot]
            remote(slot, slot, n_send.at[part, step], n_recv.at[part, spot], peer).wait_recv()

        def choose(b, carry, part=part):
            weighed = []
            for i in range(8):
                local = row * 8 + i if part == 0 else (i // 2) * 8 + column * 2 + i % 2
                named = jnp.concatenate(
                    [maps[part, b, z, pl.ds(local, 1), :] for z in range(4)], axis=1
                )
                gates = jnp.concatenate(
                    [maps[part, b, z, pl.ds(32 + local, 1), :] for z in range(4)], axis=1
                )
                hit = wanted == named
                pick[part, b, i * group : (i + 1) * group, :] = jnp.where(hit, 1.0, 0.0).astype(
                    jnp.bfloat16
                )
                weighed.append(jnp.where(hit, gates, 0.0))
            made_of = jnp.concatenate(weighed, axis=0)
            weigh_ref[part, b] = made_of.T.astype(jnp.bfloat16)
            return carry

        lax.fori_loop(0, 4, choose, 0)

    mine = (column * 2 + core, row * 2 + core)
    owns = []
    for q, (start, size, planes_first, part) in enumerate(chunks):
        _, (second, _) = hops(planes_first, part, at, where)
        for step in (1, 2, 3):
            peer, spot = second(step)
            slot = tokens[q].at[spot] if planes_first else tokens[q].at[:, spot]
            remote(slot, slot, b_send.at[q, step], b_recv.at[q, spot], peer).wait_recv()

        def gather(b, carry, q=q, part=part, size=size):
            rows = tokens[q][b].reshape(width, size)
            chosen = jnp.dot(pick[part, b], rows, preferred_element_type=jnp.float32)
            outbox[q][:, b] = chosen.astype(jnp.bfloat16).reshape(8, group, size)
            return carry

        lax.fori_loop(0, 4, gather, 0)
        cols = pl.ds(start, size)
        target = inbox.at[:, column, core, :, cols] if part == 0 else inbox.at[row, :, core, :, cols]
        for step in (2, 3, 4, 5, 6, 7, 1):
            peer, spot = swap_peer(part, step, where)
            send(remote(
                outbox[q].at[spot], target, c_send.at[q, step], c_recv.at[q, mine[part]], peer
            ))
        own = pltpu.make_async_copy(outbox[q].at[mine[part]], target, local_sem.at[q])
        own.start()
        owns.append(own)

    def arrive(which):
        for q in which:
            start, size, planes_first, part = chunks[q]
            cols = pl.ds(start, size)
            owns[q].wait()
            for step in range(1, 8):
                peer, spot = swap_peer(part, step, where)
                if part == 0:
                    slot = inbox.at[:, spot // 2, spot % 2, :, cols]
                else:
                    slot = inbox.at[spot // 2, :, spot % 2, :, cols]
                remote(
                    outbox[q].at[spot], slot, c_send.at[q, step], c_recv.at[q, spot], peer
                ).wait_recv()

    early = chunks[EARLY][0]
    hidden_width = w_gate.shape[1]
    arrive(range(EARLY))
    for load in loads:
        load.wait()

    def begin(r, carry):
        x = inbox[r, :, :, :, 0:early].reshape(8 * group, early)
        partial[r, :, 0:hidden_width] = jnp.dot(
            x, w_gate[0:early, :], preferred_element_type=jnp.float32
        )
        partial[r, :, hidden_width:] = jnp.dot(
            x, w_up[0:early, :], preferred_element_type=jnp.float32
        )
        return carry

    lax.fori_loop(0, 4, begin, 0)
    for q in range(EARLY, COUNT - 1):
        arrive((q,))
        low, high = chunks[q][0], chunks[q + 1][0]

        def resume(r, carry, low=low, high=high):
            x = inbox[r, :, :, :, low:high].reshape(8 * group, high - low)
            partial[r, :, 0:hidden_width] += jnp.dot(
                x, w_gate[low:high, :], preferred_element_type=jnp.float32
            )
            partial[r, :, hidden_width:] += jnp.dot(
                x, w_up[low:high, :], preferred_element_type=jnp.float32
            )
            return carry

        lax.fori_loop(0, 4, resume, 0)
    arrive((COUNT - 1,))
    cut = chunks[COUNT - 1][0]

    def expert(r, carry):
        x = inbox[r, :, :, :, cut:].reshape(8 * group, inbox.shape[-1] - cut)
        gate = partial[r, :, 0:hidden_width] + jnp.dot(
            x, w_gate[cut:, :], preferred_element_type=jnp.float32
        )
        up = partial[r, :, hidden_width:] + jnp.dot(
            x, w_up[cut:, :], preferred_element_type=jnp.float32
        )
        hidden = (gate / (1.0 + jnp.exp(-gate)) * up).astype(jnp.bfloat16)
        out = jnp.dot(hidden, w_down[...], preferred_element_type=jnp.float32)

        @pl.when(r >= 2)
        def _():
            pltpu.make_async_copy(made.at[r % 2], made_ref.at[r - 2], made_sem.at[r % 2]).wait()

        made[r % 2] = out.astype(jnp.bfloat16).reshape(made.shape[1:])
        pltpu.make_async_copy(made.at[r % 2], made_ref.at[r], made_sem.at[r % 2]).start()
        return carry

    lax.fori_loop(0, 4, expert, 0)
    for r in (2, 3):
        pltpu.make_async_copy(made.at[r % 2], made_ref.at[r], made_sem.at[r % 2]).wait()
    for copy in sent:
        copy.wait_send()


def serve(rows, maps, w_gate, w_up, w_down, capacity):
    tokens, width = rows.shape
    hidden = w_gate.shape[2]
    sizes = [size for _, size, _, _ in spans(width)]
    group = 4 * capacity
    bf = jnp.bfloat16
    dma = pltpu.SemaphoreType.DMA
    vmem = pl.BlockSpec(memory_space=pltpu.VMEM)
    anywhere = pl.BlockSpec(memory_space=pl.ANY)
    return pl.pallas_call(
        serve_body,
        out_shape=(
            jax.ShapeDtypeStruct((4, 4, 2, group, width), bf),
            jax.ShapeDtypeStruct((2, 4, 4 * tokens, 8 * group), bf),
        ),
        in_specs=[vmem, vmem, anywhere, anywhere, anywhere],
        out_specs=(anywhere, vmem),
        scratch_shapes=[
            [pltpu.VMEM((4, 4, tokens, size), bf) for size in sizes],
            pltpu.VMEM((2, 4, 4) + maps.shape[1:], jnp.float32),
            pltpu.VMEM((2, 4, 8 * group, 4 * tokens), bf),
            [pltpu.VMEM((8, 4, group, size), bf) for size in sizes],
            pltpu.VMEM((4, 4, 2, group, width), bf),
            pltpu.VMEM((width, hidden), bf),
            pltpu.VMEM((width, hidden), bf),
            pltpu.VMEM((hidden, width), bf),
            pltpu.VMEM((4, 8 * group, 2 * hidden), jnp.float32),
            pltpu.VMEM((2, 4, 2, group, width), bf),
            dma((COUNT, 4)), dma((COUNT, 4)),
            dma((COUNT, 4)), dma((COUNT, 4)),
            dma((COUNT, 8)), dma((COUNT, 8)),
            dma((2, 4)), dma((2, 4)), dma((2, 4)), dma((2, 4)),
            dma((COUNT,)), dma((3,)), dma((2,)),
        ],
        compiler_params=pltpu.CompilerParams(
            collective_id=0, has_side_effects=True, vmem_limit_bytes=63 << 20
        ),
        name="serve",
    )(rows, maps, w_gate, w_up, w_down)


def combine_body(
    made_ref, weigh_ref, base_ref, out_ref,
    back, share, shares, total, totals,
    c_send, c_recv, b_send, b_recv, f_send, f_recv, local_sem,
):
    where = place()
    plane, row, column, core = where
    at = (row, column)
    mine = (column * 2 + core, row * 2 + core)
    tokens = base_ref.shape[0]
    forward = tuple(spans(base_ref.shape[1]))
    chunks = tuple((q, forward[q]) for q in BACKWARD)
    greet(where)
    sent = []

    def send(copy):
        copy.start()
        sent.append(copy)

    for q, (start, size, planes_first, part) in chunks:
        cols = pl.ds(start, size)

        def source(spot):
            if part == 0:
                return made_ref.at[:, spot // 2, spot % 2, :, cols]
            return made_ref.at[spot // 2, :, spot % 2, :, cols]

        for step in (2, 3, 4, 5, 6, 7, 1):
            peer, spot = swap_peer(part, step, where)
            send(remote(
                source(spot), back[q].at[:, mine[part]],
                c_send.at[q, step], c_recv.at[q, mine[part]], peer,
            ))
        pltpu.make_async_copy(
            source(mine[part]), back[q].at[:, mine[part]], local_sem.at[q]
        ).start()
    for q, (start, size, planes_first, part) in chunks:
        for step in range(1, 8):
            peer, spot = swap_peer(part, step, where)
            slot = back[q].at[:, spot]
            remote(slot, slot, c_send.at[q, step], c_recv.at[q, spot], peer).wait_recv()
        slot = back[q].at[:, mine[part]]
        pltpu.make_async_copy(slot, slot, local_sem.at[q]).wait()

        def weigh(b, carry, q=q, part=part, size=size):
            rows = back[q][b].reshape(weigh_ref.shape[-1], size)
            summed = jnp.dot(weigh_ref[part, b], rows, preferred_element_type=jnp.float32)
            share[q][b] = summed.astype(jnp.bfloat16).reshape(4, tokens, size)
            return carry

        lax.fori_loop(0, 4, weigh, 0)
        _, (second, here) = hops(planes_first, part, at, where)
        for step in (1, 2, 3):
            peer, spot = second(step)
            slot = share[q].at[spot] if planes_first else share[q].at[:, spot]
            send(remote(
                slot, shares[q].at[here], b_send.at[q, step], b_recv.at[q, here], peer
            ))
    for q, (start, size, planes_first, part) in chunks:
        (first, near), (second, here) = hops(planes_first, part, at, where)
        added = share[q][here] if planes_first else share[q][:, here]
        added = added.astype(jnp.float32)
        for step in (1, 2, 3):
            peer, spot = second(step)
            slot = shares[q].at[spot]
            remote(slot, slot, b_send.at[q, step], b_recv.at[q, spot], peer).wait_recv()
            added = added + shares[q][spot].astype(jnp.float32)
        total[q][...] = added.astype(jnp.bfloat16)
        for step in (1, 2, 3):
            peer, spot = first(step)
            send(remote(
                total[q].at[spot], totals[q].at[near],
                f_send.at[q, step], f_recv.at[q, near], peer,
            ))
    for q, (start, size, planes_first, part) in chunks:
        (first, near), _ = hops(planes_first, part, at, where)
        cols = slice(start, start + size)
        added = total[q][near].astype(jnp.float32)
        for step in (1, 2, 3):
            peer, spot = first(step)
            slot = totals[q].at[spot]
            remote(slot, slot, f_send.at[q, step], f_recv.at[q, spot], peer).wait_recv()
            added = added + totals[q][spot].astype(jnp.float32)
        out_ref[:, cols] = (base_ref[:, cols].astype(jnp.float32) + added).astype(jnp.bfloat16)
    for copy in sent:
        copy.wait_send()


def combine(made, weigh, base):
    tokens, width = base.shape
    sizes = [size for _, size, _, _ in spans(width)]
    group = made.shape[3]
    bf = jnp.bfloat16
    dma = pltpu.SemaphoreType.DMA
    vmem = pl.BlockSpec(memory_space=pltpu.VMEM)
    return pl.pallas_call(
        combine_body,
        out_shape=jax.ShapeDtypeStruct(base.shape, bf),
        in_specs=[pl.BlockSpec(memory_space=pl.ANY), vmem, vmem],
        out_specs=vmem,
        scratch_shapes=[
            [pltpu.VMEM((4, 8, group, size), bf) for size in sizes],
            [pltpu.VMEM((4, 4, tokens, size), bf) for size in sizes],
            [pltpu.VMEM((4, 4, tokens, size), bf) for size in sizes],
            [pltpu.VMEM((4, tokens, size), bf) for size in sizes],
            [pltpu.VMEM((4, tokens, size), bf) for size in sizes],
            dma((COUNT, 8)), dma((COUNT, 8)),
            dma((COUNT, 4)), dma((COUNT, 4)),
            dma((COUNT, 4)), dma((COUNT, 4)), dma((COUNT,)),
        ],
        compiler_params=pltpu.CompilerParams(
            collective_id=1, has_side_effects=True, vmem_limit_bytes=62 << 20
        ),
        name="combine",
    )(made, weigh, base)


def routing_maps(routes, gates, experts, planes):
    rows = routes.shape[0]
    ids = routes.T[None, :, :]
    hit = ids == jnp.arange(experts, dtype=jnp.int32)[:, None, None]
    named = jnp.sum(hit.astype(jnp.float32), axis=1)
    weight = jnp.sum(jnp.where(hit, gates.T[None, :, :], 0.0), axis=1)
    upto = (
        jnp.arange(rows, dtype=jnp.int32)[:, None] <= jnp.arange(rows, dtype=jnp.int32)[None, :]
    )
    order = jnp.dot(
        named.astype(jnp.bfloat16), upto.astype(jnp.bfloat16), preferred_element_type=jnp.float32
    )
    slot = order * named
    per_plane = experts // planes
    return jnp.concatenate(
        [slot.reshape(planes, per_plane, rows), weight.reshape(planes, per_plane, rows)], axis=1
    )


def front_body(
    exp_scale, length_ref, tokens_ref, gain_ref, wq_ref, wk_ref, wv_ref, cos_ref, sin_ref,
    q_gain_ref, k_gain_ref, ck_ref, cv_ref, wo_ref, moe_gain_ref,
    after_ref, moe_ref, fk_ref, fv_ref,
    weights, w_out, normed, proj, queries, kaug, vaug, attended, share, shares,
    s_send, s_recv, t_send, t_recv, x_send, x_recv, z_send, z_recv, cache_sem,
):
    where = place()
    plane, row, column, core = where
    stretch_len = tokens_ref.shape[0]
    width = q_gain_ref.shape[1]
    heads = queries.shape[0]
    cached = ck_ref.shape[1]
    fresh = fk_ref.shape[0]
    block = stretch_len // 4
    caches = [
        pltpu.make_async_copy(src.at[0], dst.at[0:cached, 0:width], cache_sem.at[i])
        for i, (src, dst) in enumerate(((ck_ref, kaug), (cv_ref, vaug)))
    ]
    for copy in caches:
        copy.start()
    q_cols = wq_ref.shape[1]
    k_cols = wk_ref.shape[1]
    weights[row, column, core, :, 0:q_cols] = wq_ref[...]
    weights[row, column, core, :, q_cols : q_cols + k_cols] = wk_ref[...]
    weights[row, column, core, :, q_cols + k_cols :] = wv_ref[...]
    w_out[row, column, core] = wo_ref[...]
    greet(where)
    sent = []

    def send(copy):
        copy.start()
        sent.append(copy)

    arrays = (weights, w_out)

    def half(array, part):
        middle = array.shape[-1] // 2
        return slice(0, middle) if part == 0 else slice(middle, 2 * middle)

    def near(n, part, spot_row, spot_column, side):
        return arrays[n].at[spot_row, spot_column, side, :, half(arrays[n], part)]

    def line(n, part, spot):
        if part == 0:
            return arrays[n].at[:, spot, core, :, half(arrays[n], part)]
        return arrays[n].at[spot, :, core, :, half(arrays[n], part)]

    at = (row, column)
    across = (column, row)
    for n in range(2):
        for part in range(2):
            for step in (1, 2, 3):
                peer, spot = ring_peer(part, step, where)
                slot = near(n, part, row, column, core)
                send(remote(
                    slot, slot, s_send.at[n, part, step], s_recv.at[n, part, at[part]], peer
                ))

    def second_stage(n):
        for part in range(2):
            for step in (1, 2, 3):
                peer, spot = ring_peer(part, step, where)
                slot = near(n, part, spot, column, core) if part == 0 else near(
                    n, part, row, spot, core
                )
                remote(
                    slot, slot, s_send.at[n, part, step], s_recv.at[n, part, spot], peer
                ).wait_recv()
            for step in (1, 2, 3):
                peer, spot = ring_peer(1 - part, step, where)
                slot = line(n, part, across[part])
                send(remote(
                    slot, slot, t_send.at[n, part, step], t_recv.at[n, part, across[part]], peer
                ))

    def hand_over(n):
        for part in range(2):
            for step in (1, 2, 3):
                peer, spot = ring_peer(1 - part, step, where)
                slot = line(n, part, spot)
                remote(
                    slot, slot, t_send.at[n, part, step], t_recv.at[n, part, spot], peer
                ).wait_recv()
            peer, _ = swap_peer(0, 1, where)
            slot = arrays[n].at[:, :, core, :, half(arrays[n], part)]
            pair(n, part).start()

    def pair(n, part):
        peer, _ = swap_peer(0, 1, where)
        slot = arrays[n].at[:, :, core, :, half(arrays[n], part)]
        return remote(slot, slot, x_send.at[n, part], x_recv.at[n, part], peer)

    def handed(n):
        for part in range(2):
            peer, _ = swap_peer(0, 1, where)
            slot = arrays[n].at[:, :, 1 - core, :, half(arrays[n], part)]
            remote(slot, slot, x_send.at[n, part], x_recv.at[n, part], peer).wait_recv()

    def normalize(i, carry):
        rows = pl.ds(i * block, block)
        values = tokens_ref[rows, :].astype(jnp.float32)
        factor = lax.rsqrt(jnp.mean(values * values, axis=-1, keepdims=True) + EPS)
        normed[rows, :] = (values * factor * gain_ref[...]).astype(jnp.bfloat16)
        return carry

    lax.fori_loop(0, 4, normalize, 0)
    second_stage(0)
    span = cached + fresh
    position = lax.broadcasted_iota(jnp.int32, (span, width), 0)
    lane = lax.broadcasted_iota(jnp.int32, (span, width), 1)
    hidden = (lane == 0) & (position >= length_ref[0]) & (position < cached)
    kaug[:, width:] = jnp.where(hidden, -1e30, 0.0).astype(jnp.bfloat16)
    vaug[:, width:] = jnp.ones((span, width), jnp.bfloat16)
    hand_over(0)
    second_stage(1)
    handed(0)

    flat = weights[...].reshape(normed.shape[1], weights.shape[-1])
    proj[...] = jnp.dot(normed[...], flat, preferred_element_type=jnp.float32)

    def turned(values, gain):
        factor = lax.rsqrt(jnp.mean(values * values, axis=-1, keepdims=True) + EPS)
        values = values * factor * gain
        swapped = pltpu.roll(values, width // 2, 1)
        return (values * cos_ref[...] + swapped * sin_ref[...]).astype(jnp.bfloat16)

    for head in range(heads):
        queries[head] = turned(proj[:, head * width : (head + 1) * width], q_gain_ref[...])
    new_keys = turned(proj[:, q_cols : q_cols + k_cols], k_gain_ref[...])
    new_values = proj[:, q_cols + k_cols :].astype(jnp.bfloat16)
    fk_ref[...] = new_keys
    fv_ref[...] = new_values
    for copy in caches:
        copy.wait()
    kaug[cached:, 0:width] = new_keys
    vaug[cached:, 0:width] = new_values

    dims = (((1,), (1,)), ((), ()))
    count = heads * block

    def attend(spot):
        own = queries[:, pl.ds(spot * block, block), :].reshape(count, width)
        widened = jnp.concatenate([own, jnp.ones((count, width), jnp.bfloat16)], axis=1)
        old = lax.dot_general(widened, kaug[0:cached, :], dims, preferred_element_type=jnp.float32)
        new = lax.dot_general(
            own, kaug[cached:, 0:width], dims, preferred_element_type=jnp.float32
        )
        token = lax.broadcasted_iota(jnp.int32, (count, fresh), 0) % block + spot * block
        new = jnp.where(lax.broadcasted_iota(jnp.int32, (count, fresh), 1) <= token, new, -1e30)
        peak = jnp.maximum(
            jnp.max(old, axis=1, keepdims=True), jnp.max(new, axis=1, keepdims=True)
        )
        old = jnp.exp2((old - peak) * exp_scale).astype(jnp.bfloat16)
        new = jnp.exp2((new - peak) * exp_scale).astype(jnp.bfloat16)
        mixed = jnp.dot(old, vaug[0:cached, :], preferred_element_type=jnp.float32) + jnp.dot(
            new, vaug[cached:, :], preferred_element_type=jnp.float32
        )
        mixed = (mixed[:, :width] / mixed[:, width:]).astype(jnp.bfloat16)
        for head in range(heads):
            attended[spot, :, head * width : (head + 1) * width] = mixed[
                head * block : (head + 1) * block
            ]

    def project_out(spot):
        flat = w_out[...].reshape(attended.shape[2], w_out.shape[-1])
        return jnp.dot(attended[spot], flat, preferred_element_type=jnp.float32)

    def give(i):
        spot = (plane + 1 + i) % 4
        share[spot] = project_out(spot).astype(jnp.bfloat16)
        remote(
            share.at[spot], shares.at[plane], z_send.at[spot], z_recv.at[plane],
            (spot, row * 8 + column * 2 + core),
        ).start()

    def turn(i, carry):
        attend((plane + 1 + i) % 4)

        @pl.when(i == 0)
        def _():
            hand_over(1)

        @pl.when(i == 1)
        def _():
            handed(1)
            give(0)

        @pl.when((i > 0) & (i < 3))
        def _():
            give(i)

        return carry

    lax.fori_loop(0, 4, turn, 0)
    added = project_out(plane)
    for step in (1, 2, 3):
        peer, spot = plane_peer(step, where)
        remote(
            share.at[spot], shares.at[spot], z_send.at[spot], z_recv.at[spot], peer
        ).wait_recv()
        added = added + shares[spot].astype(jnp.float32)
    resident = tokens_ref[pl.ds(pl.multiple_of(plane * block, block), block), :]
    after = (resident.astype(jnp.float32) + added).astype(jnp.bfloat16)
    after_ref[...] = after
    values = after.astype(jnp.float32)
    factor = lax.rsqrt(jnp.mean(values * values, axis=-1, keepdims=True) + EPS)
    moe_ref[...] = (values * factor * moe_gain_ref[...]).astype(jnp.bfloat16)
    for copy in sent:
        copy.wait_send()
    for n in range(2):
        for part in range(2):
            pair(n, part).wait_send()
    for step in (1, 2, 3):
        peer, spot = plane_peer(step, where)
        remote(
            share.at[spot], shares.at[spot], z_send.at[spot], z_recv.at[spot], peer
        ).wait_send()


def front(
    length, tokens, attn_gain, w_query, w_key, w_value, cosine, sine, q_gain, k_gain,
    cache_keys, cache_values, w_out, moe_gain,
):
    stretch_len, model_width = tokens.shape
    width = q_gain.shape[0]
    heads = w_query.shape[1] // width
    columns = w_query.shape[1] + w_key.shape[1] + w_value.shape[1]
    span = cache_keys.shape[1] + stretch_len
    block = stretch_len // 4
    bf = jnp.bfloat16
    dma = pltpu.SemaphoreType.DMA
    vmem = pl.BlockSpec(memory_space=pltpu.VMEM)
    anywhere = pl.BlockSpec(memory_space=pl.ANY)
    return pl.pallas_call(
        functools.partial(front_body, width ** -0.5 * math.log2(math.e)),
        out_shape=(
            jax.ShapeDtypeStruct((block, model_width), bf),
            jax.ShapeDtypeStruct((block, model_width), bf),
            jax.ShapeDtypeStruct((stretch_len, width), bf),
            jax.ShapeDtypeStruct((stretch_len, width), bf),
        ),
        in_specs=[pl.BlockSpec(memory_space=pltpu.SMEM)] + [vmem] * 9 + [anywhere] * 2 + [vmem] * 2,
        out_specs=(vmem,) * 4,
        scratch_shapes=[
            pltpu.VMEM((4, 4, 2, w_query.shape[0], columns), bf),
            pltpu.VMEM((4, 4, 2, w_out.shape[0], model_width), bf),
            pltpu.VMEM((stretch_len, model_width), bf),
            pltpu.VMEM((stretch_len, columns), jnp.float32),
            pltpu.VMEM((heads, stretch_len, width), bf),
            pltpu.VMEM((span, 2 * width), bf),
            pltpu.VMEM((span, 2 * width), bf),
            pltpu.VMEM((4, block, heads * width), bf),
            pltpu.VMEM((4, block, model_width), bf),
            pltpu.VMEM((4, block, model_width), bf),
            dma((2, 2, 4)), dma((2, 2, 4)), dma((2, 2, 4)), dma((2, 2, 4)),
            dma((2, 2)), dma((2, 2)), dma((4,)), dma((4,)), dma((2,)),
        ],
        compiler_params=pltpu.CompilerParams(
            collective_id=2, has_side_effects=True, vmem_limit_bytes=63 << 20
        ),
        name="front",
    )(
        length, tokens, attn_gain[None], w_query, w_key, w_value, cosine, sine,
        q_gain[None], k_gain[None], cache_keys, cache_values, w_out, moe_gain[None],
    )


def turning(length, stretch_len, width):
    half_dim = width // 2
    frequency = THETA ** (-jnp.arange(half_dim, dtype=jnp.float32) * 2.0 / width)
    positions = length + jnp.arange(stretch_len, dtype=jnp.int32)
    angles = positions.astype(jnp.float32)[:, None] * frequency[None, :]
    cosine, sine = jnp.cos(angles), jnp.sin(angles)
    return jnp.concatenate([cosine, cosine], axis=1), jnp.concatenate([-sine, sine], axis=1)


def append_body(length_ref, ck_ref, cv_ref, fk_ref, fv_ref, ko_ref, vo_ref, moved):
    length = length_ref[0]
    cached = ck_ref.shape[1]
    fresh = fk_ref.shape[0]
    row = lax.broadcasted_iota(jnp.int32, ck_ref.shape[1:], 0)
    for cache, new, out in ((ck_ref, fk_ref, ko_ref), (cv_ref, fv_ref, vo_ref)):
        moved[...] = jnp.zeros_like(moved)
        moved[pl.ds(length, fresh), :] = new[...].astype(jnp.float32)
        tail = moved[...].astype(jnp.bfloat16)
        out[0, 0:cached] = jnp.where(row < length, cache[0], tail[0:cached])
        out[0, cached:] = tail[cached:]


def append(cache_keys, cache_values, fresh_keys, fresh_values, length):
    _, cached, width = cache_keys.shape
    span = cached + fresh_keys.shape[0]
    vmem = pl.BlockSpec(memory_space=pltpu.VMEM)
    return pl.pallas_call(
        append_body,
        out_shape=(jax.ShapeDtypeStruct((1, span, width), jnp.bfloat16),) * 2,
        in_specs=[pl.BlockSpec(memory_space=pltpu.SMEM)] + [vmem] * 4,
        out_specs=(vmem, vmem),
        scratch_shapes=[pltpu.VMEM((span, width), jnp.float32)],
        compiler_params=pltpu.CompilerParams(vmem_limit_bytes=32 << 20),
        name="append",
    )(length, cache_keys, cache_values, fresh_keys, fresh_values)


def body(
    hidden_in,
    cache_keys,
    cache_values,
    cache_len,
    attn_gain,
    w_query,
    w_key,
    w_value,
    q_gain,
    k_gain,
    w_out,
    moe_gain,
    expert_ids,
    expert_gates,
    w_gate,
    w_up,
    w_down,
):
    tokens = hidden_in[0]
    stretch_len = tokens.shape[0]
    length = cache_len[0]
    groups = lax.axis_size("req")
    row_count = stretch_len // groups
    cosine, sine = turning(length, stretch_len, q_gain.shape[0])
    after_attn, moe_in, fresh_keys, fresh_values = front(
        cache_len, tokens, attn_gain, w_query, w_key, w_value, cosine, sine, q_gain, k_gain,
        cache_keys, cache_values, w_out, moe_gain,
    )
    routes = expert_ids[0]
    top_k = routes.shape[1]
    experts = groups * lax.axis_size("exp")
    capacity = 3 * top_k * row_count // (2 * experts)
    maps = routing_maps(routes, expert_gates[0], experts, groups)
    made, weigh = serve(moe_in, maps, w_gate, w_up, w_down, capacity)
    result_rows = combine(made, weigh, after_attn)
    keys_out, values_out = append(
        cache_keys, cache_values, fresh_keys, fresh_values, cache_len
    )
    return (result_rows[None], keys_out, values_out)


def solution(mesh):
    placed = (
        P("exp", None, None),
        P("exp", None, "req"),
        P("exp", None, "req"),
        P("exp"),
        P(),
        P("exp", "req"),
        P("exp", "req"),
        P("exp", "req"),
        P(),
        P(),
        P(("req", "exp"), None),
        P(),
        P("exp", "req", None),
        P("exp", "req", None),
        P(("req", "exp"), None, None),
        P(("req", "exp"), None, None),
        P(("req", "exp"), None, None),
    )
    return jax.shard_map(
        body,
        mesh=mesh,
        in_specs=placed,
        out_specs=(P("exp", "req", None), P("exp", None, "req"), P("exp", None, "req")),
        check_vma=False,
    )
```
